512 devices in a mesh: ctx: 16 (over z_lo, core), tp: 4 (over x), dp: 8 (over y, z_hi).
Axes of the slice: x: 4, y: 4, z: 16 (z_hi: 2, z_lo: 8; z = z_hi * 8 + z_lo), core: 2. Of those that a mesh axis runs over, the one named last changes fastest.
Arguments:
- queries: bfloat16 [8192, 8192], P(('dp', 'ctx'), 'tp'), parts along dimension 0, may hold values from -12 to 12
- cache_keys: bfloat16 [65536, 1024], P(('dp', 'ctx'), 'tp'), parts along dimension 0, may hold values from -4 to 4
- cache_values: bfloat16 [65536, 1024], P(('dp', 'ctx'), 'tp'), parts along dimension 0, may hold values from -6 to 6
- new_keys: bfloat16 [8192, 1024], P(('dp', 'ctx'), 'tp'), parts along dimension 0, may hold values from -6 to 6
- new_values: bfloat16 [8192, 1024], P(('dp', 'ctx'), 'tp'), parts along dimension 0, may hold values from -6 to 6
- prefix_len: int32 [8], P('dp'), parts along dimension 0, may hold values from 4096 to 8192
Outputs:
- attended: bfloat16 [8192, 8192], P(('dp', 'ctx'), 'tp'), parts along dimension 0
The draws below stay inside these ranges and needn't reach their ends.
There are 8 independent parts, one for each index of `dp`. The reference program is written for one: setup_inputs(seed, part) draws one part's arguments, and reference() takes and returns one part's arrays. A program takes and returns all parts, laid end to end along the dimension named above; each array names one. Nothing has to cross between parts.
All inputs are finite; a program needn't handle non-finite values.
Results may differ from the reference program's by a relative error of at most 0.038.
Values may be sent and summed in bfloat16 or wider, within the bound.
A program may use at most 64 MiB of HBM per device.

```python
import jax
import jax.numpy as jnp
from jax import lax

HEADS = 64
KV_HEADS = 8
HEAD_DIM = 128
GROUP = 8
SPAN = 1024
CACHE = 8192


def draw_queries(key, part):
    drawn = 2.0 * jnp.clip(jax.random.normal(jax.random.fold_in(key, 12), (SPAN, HEADS * HEAD_DIM), jnp.float32), -6.0, 6.0)
    return drawn.astype(jnp.bfloat16)


def draw_cache_keys(key, part):
    drawn = jnp.clip(jax.random.normal(jax.random.fold_in(key, 22), (CACHE, KV_HEADS * HEAD_DIM), jnp.float32), -4.0, 4.0)
    return drawn.astype(jnp.bfloat16)


def block_scale(stream_key, shape, pieces, least, high):
    gain, own = 1.0, jax.random.fold_in(stream_key, 6)
    for axis_at, shards_of in pieces:
        draws = jnp.exp(jax.random.uniform(jax.random.fold_in(own, axis_at), (shards_of,), jnp.float32, least / len(pieces), high / len(pieces)))
        gain = gain * jnp.repeat(draws, shape[axis_at] // shards_of).reshape([-1 if axis == axis_at else 1 for axis in range(len(shape))])
    return gain


def noise(rng, extent, deviation, reach, cuts=(), held_as=jnp.bfloat16):
    values = jax.random.normal(rng, extent, jnp.float32) * deviation
    if len(cuts) > 0:
        values = block_scale(rng, extent, cuts, -0.22, 0.18) * values
    return jnp.clip(values, min=-reach, max=reach).astype(held_as)


def setup_inputs(seed: int = 0, part: int = 0) -> dict:
    streams_of = jax.random.split(jax.random.key(seed), 7)
    part_splits = jax.random.split(jax.random.fold_in(streams_of[6], part), 7)
    queries = draw_queries(jax.random.fold_in(jax.random.fold_in(streams_of[6], part), 71), part)
    cache_keys = draw_cache_keys(jax.random.fold_in(jax.random.fold_in(streams_of[6], part), 71), part)
    cache_values = noise(part_splits[2], (CACHE, KV_HEADS * HEAD_DIM), 1.0, 6.0, ((0, 16), (1, 4)))
    new_keys = noise(part_splits[3], (SPAN, KV_HEADS * HEAD_DIM), 1.0, 6.0, ((0, 16), (1, 4)))
    new_values = noise(part_splits[4], (SPAN, KV_HEADS * HEAD_DIM), 1.0, 6.0, ((0, 16), (1, 4)))
    prefix_len = jax.random.randint(part_splits[5], (1,), CACHE // 2, CACHE + 1).astype(jnp.int32)
    return {"queries": queries, "cache_keys": cache_keys, "cache_values": cache_values, "new_keys": new_keys, "new_values": new_values, "prefix_len": prefix_len}


def reference(queries, cache_keys, cache_values, new_keys, new_values, prefix_len):
    length = prefix_len[0]
    all_rows = CACHE + SPAN
    all_keys = jnp.concatenate([cache_keys, new_keys], 0)
    all_values = jnp.concatenate([cache_values, new_values], 0)
    key_index = jnp.arange(all_rows, dtype=jnp.int32)
    query_pos = jnp.arange(SPAN, dtype=jnp.int32)
    allowed = jnp.where(key_index[None, :] < CACHE, key_index[None, :] < length,
                        (key_index[None, :] - CACHE) <= query_pos[:, None])
    grouped = queries.reshape(SPAN, KV_HEADS, GROUP, HEAD_DIM).transpose(1, 0, 2, 3)
    key_heads = all_keys.reshape(all_rows, KV_HEADS, HEAD_DIM).transpose(1, 0, 2)
    value_heads = all_values.reshape(all_rows, KV_HEADS, HEAD_DIM).transpose(1, 0, 2)
    scale = HEAD_DIM ** -0.5

    def one_head(head_inputs):
        query_part, key_part, value_part = head_inputs
        scores = jnp.einsum('cpd,kd->cpk', query_part.astype(jnp.float32), key_part.astype(jnp.float32)) * scale
        scores = jnp.where(allowed[:, None, :], scores, jnp.float32(-1e30))
        largest = jnp.max(scores, -1, keepdims=True)
        weights = jnp.where(allowed[:, None, :], jnp.exp(scores - largest), jnp.float32(0.0))
        denominator = jnp.sum(weights, -1)
        rounded = lax.optimization_barrier(weights.astype(jnp.bfloat16))
        numerator = jnp.einsum('cpk,kd->cpd', rounded.astype(jnp.float32), value_part.astype(jnp.float32))
        return numerator / denominator[..., None]

    result = lax.map(one_head, (grouped, key_heads, value_heads))
    return result.transpose(1, 0, 2, 3).reshape(SPAN, HEADS * HEAD_DIM).astype(jnp.bfloat16)
```

```python
import functools

import jax
import jax.numpy as jnp
from jax import lax
from jax.experimental import pallas as pl
from jax.experimental.pallas import tpu as pltpu
from jax.sharding import PartitionSpec as P

HEAD_DIM = 128
LOG2_E = 1.4426950408889634
MASKED = -1e30
TILE = 256


def kernel(chips, length_ref, q_ref, ck_ref, cv_ref, nk_ref, nv_ref, out_ref,
           held, qs, tops, totals, acc, local_sem, left_sem, right_sem, mate_sem, recv_sem):
    me = lax.axis_index("ctx")
    chip = me // 2
    core = me % 2
    cache_rows = ck_ref.shape[0]
    new_rows = nk_ref.shape[0]
    key_rows = cache_rows + new_rows
    width = ck_ref.shape[1]
    tiles = qs.shape[0]
    tiles_per_kv = tiles // (width // HEAD_DIM)
    heads = q_ref.shape[1] // HEAD_DIM
    heads_per_tile = TILE // new_rows
    length = length_ref[0]
    scale = (HEAD_DIM ** -0.5) * LOG2_E

    loads = []
    for n, (src, first, rows) in enumerate((
        (ck_ref, 0, cache_rows), (nk_ref, cache_rows, new_rows),
        (cv_ref, key_rows, cache_rows), (nv_ref, key_rows + cache_rows, new_rows),
    )):
        load = pltpu.make_async_copy(src, held.at[me, pl.ds(first, rows)], local_sem.at[n])
        load.start()
        loads.append(load)

    barrier = pltpu.get_barrier_semaphore()
    pl.semaphore_signal(barrier, inc=1, device_id={"ctx": chip * 2 + 1 - core})

    @pl.when(chip > 0)
    def _():
        pl.semaphore_signal(barrier, inc=1, device_id={"ctx": me - 2})

    @pl.when(chip < chips - 1)
    def _():
        pl.semaphore_signal(barrier, inc=1, device_id={"ctx": me + 2})

    pl.semaphore_wait(
        barrier, 1 + (chip > 0).astype(jnp.int32) + (chip < chips - 1).astype(jnp.int32))

    def copy_of(block, half, sems, target):
        part = held.at[block, pl.ds(half * key_rows, key_rows)]
        return pltpu.make_async_remote_copy(
            src_ref=part, dst_ref=part, send_sem=sems.at[block // 2, half],
            recv_sem=recv_sem.at[block, half], device_id={"ctx": target})

    def to_left(block, half):
        return copy_of(block, half, left_sem, me - 2)

    def to_right(block, half):
        return copy_of(block, half, right_sem, me + 2)

    def to_mate(block, half):
        return copy_of(block, half, mate_sem, chip * 2 + 1 - core)

    def compute(block):
        def one_tile(n, carry):
            col = pl.multiple_of((n // tiles_per_kv) * HEAD_DIM, HEAD_DIM)
            keys = held[block, 0:key_rows, pl.ds(col, HEAD_DIM)]
            values = held[block, key_rows:2 * key_rows, pl.ds(col, HEAD_DIM)]
            scores = lax.dot_general(
                keys, qs[n], (((1,), (1,)), ((), ())),
                preferred_element_type=jnp.float32) * scale
            row = lax.broadcasted_iota(jnp.int32, (cache_rows, TILE), 0)
            cached = jnp.where(row + block * cache_rows < length, scores[:cache_rows], MASKED)
            new_row = lax.broadcasted_iota(jnp.int32, (new_rows, TILE), 0)
            token = lax.broadcasted_iota(jnp.int32, (new_rows, TILE), 1) % new_rows
            fresh = jnp.where(
                new_row + block * new_rows <= token + me * new_rows, scores[cache_rows:], MASKED)
            old_top = tops[n]
            top = jnp.maximum(jnp.max(cached, 0, keepdims=True), jnp.max(fresh, 0, keepdims=True))
            top = jnp.maximum(old_top, top)
            weights = jnp.exp2(jnp.concatenate([cached, fresh], 0) - top)
            rescale = jnp.exp2(old_top - top)
            tops[n] = top
            totals[n] = totals[n] * rescale + jnp.sum(weights, 0, keepdims=True)
            acc[n] = acc[n] * rescale + lax.dot_general(
                values, weights.astype(jnp.bfloat16), (((0,), (0,)), ((), ())),
                preferred_element_type=jnp.float32)
            return carry

        lax.fori_loop(0, tiles, one_tile, 0)

    def meet(block):
        return to_mate(block, 0), to_mate(block, 1)

    for half in range(2):
        loads[2 * half].wait()
        loads[2 * half + 1].wait()

        @pl.when(chip > 0)
        def _():
            to_left(me, half).start()

        @pl.when(chip < chips - 1)
        def _():
            to_right(me, half).start()

        to_mate(me, half).start()

    for head in range(heads):
        tile, at = divmod(head, heads_per_tile)
        qs[tile, at * new_rows:(at + 1) * new_rows, :] = q_ref[:, head * HEAD_DIM:(head + 1) * HEAD_DIM]
    tops[...] = jnp.full_like(tops, MASKED)
    totals[...] = jnp.zeros_like(totals)
    acc[...] = jnp.zeros_like(acc)
    compute(me)

    def mates(at_chip):
        return at_chip * 2 + 1 - core

    def take(at_chip):
        def one(n, carry):
            block = at_chip * 2 + jnp.where(n == 0, core, 1 - core)

            @pl.when(n == 1)
            def _():
                for copy in meet(block):
                    copy.wait_recv()

            compute(block)
            return carry
        lax.fori_loop(0, 2, one, 0)

    for copy in meet(mates(chip)):
        copy.wait_recv()
    compute(mates(chip))

    def pass_on(step, half):
        @pl.when(chip + step < chips)
        def _():
            block = me + 2 * step
            to_mate(block, half).wait_recv()

            @pl.when(chip > 0)
            def _():
                to_left(block, half).start()

            to_mate(block, half).start()

        @pl.when(chip - step >= 0)
        def _():
            block = me - 2 * step
            to_mate(block, half).wait_recv()

            @pl.when(chip < chips - 1)
            def _():
                to_right(block, half).start()

            to_mate(block, half).start()

    def one_step(step, carry):
        for half in range(2):
            @pl.when(step < chips)
            def _():
                pass_on(step, half)

            at_chip = chip + (step - 1) if half == 0 else chip - (step - 1)

            @pl.when((step > 1) & (at_chip >= 0) & (at_chip < chips))
            def _():
                take(at_chip)
        return carry

    lax.fori_loop(1, chips + 1, one_step, 0)

    for n in range(tiles):
        result = jnp.transpose(acc[n] / totals[n]).astype(jnp.bfloat16)
        for at in range(heads_per_tile):
            head = n * heads_per_tile + at
            out_ref[:, head * HEAD_DIM:(head + 1) * HEAD_DIM] = result[at * new_rows:(at + 1) * new_rows]

    def finish(at_chip, carry):
        block = at_chip * 2 + core
        for half in range(2):
            @pl.when((chip > 0) & (at_chip >= chip))
            def _():
                to_left(block, half).wait_send()

            @pl.when((chip < chips - 1) & (at_chip <= chip))
            def _():
                to_right(block, half).wait_send()

            to_mate(block, half).wait_send()
        return carry

    lax.fori_loop(0, chips, finish, 0)


def local(queries, cache_keys, cache_values, new_keys, new_values, prefix_len):
    count = lax.axis_size("ctx")
    chips = count // 2
    rows, width = queries.shape
    kv_width = cache_keys.shape[1]
    key_rows = cache_keys.shape[0] + new_keys.shape[0]
    tiles = rows * width // (HEAD_DIM * TILE)
    dma = pltpu.SemaphoreType.DMA
    anywhere = pl.BlockSpec(memory_space=pl.ANY)
    return pl.pallas_call(
        functools.partial(kernel, chips),
        out_shape=jax.ShapeDtypeStruct((rows, width), jnp.bfloat16),
        in_specs=[pl.BlockSpec(memory_space=pltpu.SMEM), pl.BlockSpec(memory_space=pltpu.VMEM)] + [anywhere] * 4,
        out_specs=pl.BlockSpec(memory_space=pltpu.VMEM),
        scratch_shapes=[
            pltpu.VMEM((count, 2 * key_rows, kv_width), jnp.bfloat16),
            pltpu.VMEM((tiles, TILE, HEAD_DIM), jnp.bfloat16),
            pltpu.VMEM((tiles, 1, TILE), jnp.float32),
            pltpu.VMEM((tiles, 1, TILE), jnp.float32),
            pltpu.VMEM((tiles, HEAD_DIM, TILE), jnp.float32),
            dma((4,)), dma((chips, 2)), dma((chips, 2)), dma((chips, 2)), dma((count, 2)),
        ],
        compiler_params=pltpu.CompilerParams(collective_id=0, has_side_effects=True),
    )(prefix_len, queries, cache_keys, cache_values, new_keys, new_values)


def solution(mesh):
    spec = P(("dp", "ctx"), "tp")
    return jax.shard_map(
        local, mesh=mesh, in_specs=(spec,) * 5 + (P("dp"),), out_specs=spec, check_vma=False)
```

```python
import functools

import jax
import jax.numpy as jnp
from jax import lax
from jax.experimental import pallas as pl
from jax.experimental.pallas import tpu as pltpu
from jax.sharding import PartitionSpec as P

HEAD_DIM = 128
LOG2_E = 1.4426950408889634
MASKED = -1e30
TILE = 256


HELPED = 2


def kernel(chips, length_ref, q_ref, ck_ref, cv_ref, nk_ref, nv_ref, out_ref,
           held, qs, tops, totals, acc, q_in, o_in, o_out,
           local_sem, left_sem, right_sem, mate_sem, recv_sem, q_sems, o_sems, q_recv, o_recv):
    me = lax.axis_index("ctx")
    chip = me // 2
    core = me % 2
    last = chips - 1
    low, high = HELPED, last - HELPED
    inner = (chip >= low) & (chip <= high)
    helper = (chip == low) | (chip == high)
    helped_left, helped_right = chip < low, chip > high
    helped = helped_left | helped_right
    behind, ahead = chip, last - chip
    cache_rows = ck_ref.shape[0]
    new_rows = nk_ref.shape[0]
    key_rows = cache_rows + new_rows
    heads = q_ref.shape[1] // HEAD_DIM
    heads_per_tile = TILE // new_rows
    half_width = q_ref.shape[1] // 2
    length = length_ref[0]
    scale = (HEAD_DIM ** -0.5) * LOG2_E
    mate = chip * 2 + 1 - core
    my_helper = jnp.where(helped_left, low, high) * 2 + core
    my_slot = jnp.where(helped_left, chip, last - chip)

    def helped_device(slot):
        return jnp.where(chip == low, slot, last - slot) * 2 + core

    loads = []
    for part in range(4):
        cached, fresh = ((ck_ref, nk_ref), (cv_ref, nv_ref))[part % 2]
        cols = pl.ds((1 - part // 2) * HEAD_DIM, HEAD_DIM)
        pair = (
            pltpu.make_async_copy(
                cached.at[:, cols], held.at[me, part, pl.ds(0, cache_rows)], local_sem.at[2 * part]),
            pltpu.make_async_copy(
                fresh.at[:, cols], held.at[me, part, pl.ds(cache_rows, new_rows)], local_sem.at[2 * part + 1]),
        )
        for load in pair:
            load.start()
        loads.append(pair)

    barrier = pltpu.get_barrier_semaphore()

    def greet(device):
        pl.semaphore_signal(barrier, inc=1, device_id={"ctx": device})

    greet(mate)

    @pl.when(chip > 0)
    def _():
        greet(me - 2)

    @pl.when(chip < last)
    def _():
        greet(me + 2)

    far = helped & (my_slot < HELPED - 1)

    @pl.when(far)
    def _():
        greet(my_helper)

    @pl.when(helper)
    def _():
        for slot in range(HELPED - 1):
            greet(helped_device(slot))

    def as_int(flag):
        return flag.astype(jnp.int32)

    pl.semaphore_wait(
        barrier,
        1 + as_int(chip > 0) + as_int(chip < last) + as_int(far) + as_int(helper) * (HELPED - 1))

    def q_copy(slot, device):
        return pltpu.make_async_remote_copy(
            src_ref=q_ref.at[:, pl.ds(half_width, half_width)], dst_ref=q_in.at[slot],
            send_sem=q_sems.at[0], recv_sem=q_recv.at[slot], device_id={"ctx": device})

    def o_copy(slot, device):
        return pltpu.make_async_remote_copy(
            src_ref=o_out.at[slot], dst_ref=o_in, send_sem=o_sems.at[slot],
            recv_sem=o_recv.at[0], device_id={"ctx": device})

    @pl.when(helped)
    def _():
        q_copy(my_slot, my_helper).start()

    def copy_of(block, part, sems, target):
        piece = held.at[block, part]
        return pltpu.make_async_remote_copy(
            src_ref=piece, dst_ref=piece, send_sem=sems.at[block // 2, part],
            recv_sem=recv_sem.at[block, part], device_id={"ctx": target})

    def to_left(block, part):
        return copy_of(block, part, left_sem, me - 2)

    def to_right(block, part):
        return copy_of(block, part, right_sem, me + 2)

    def to_mate(block, part):
        return copy_of(block, part, mate_sem, mate)

    def goes_left(phase):
        return jnp.where(phase == 0, chip > low, chip > 0)

    def goes_right(phase):
        return jnp.where(phase == 0, chip < high, chip < last)

    def goes_mate(phase):
        return inner | (phase == 1)

    def compute(block, phase):
        def one_tile(n, carry):
            keys = held[block, 2 * phase]
            values = held[block, 2 * phase + 1]
            asker = jnp.where(n < 4, me, helped_device((n - 4) // 2))
            scores = lax.dot_general(
                keys, qs[n], (((1,), (1,)), ((), ())),
                preferred_element_type=jnp.float32) * scale
            row = lax.broadcasted_iota(jnp.int32, (cache_rows, TILE), 0)
            cached = jnp.where(row + block * cache_rows < length, scores[:cache_rows], MASKED)
            new_row = lax.broadcasted_iota(jnp.int32, (new_rows, TILE), 0)
            token = lax.broadcasted_iota(jnp.int32, (new_rows, TILE), 1) % new_rows
            fresh = jnp.where(
                new_row + block * new_rows <= token + asker * new_rows, scores[cache_rows:], MASKED)
            old_top = tops[n]
            top = jnp.maximum(jnp.max(cached, 0, keepdims=True), jnp.max(fresh, 0, keepdims=True))
            top = jnp.maximum(old_top, top)
            weights = jnp.exp2(jnp.concatenate([cached, fresh], 0) - top)
            rescale = jnp.exp2(old_top - top)
            tops[n] = top
            totals[n] = totals[n] * rescale + jnp.sum(weights, 0, keepdims=True)
            acc[n] = acc[n] * rescale + lax.dot_general(
                values, weights.astype(jnp.bfloat16), (((0,), (0,)), ((), ())),
                preferred_element_type=jnp.float32)
            return carry

        first = jnp.where(phase == 0, 2, 0)
        end = jnp.where(phase == 0, jnp.where(helper, 4 + 2 * HELPED, jnp.where(inner, 4, 2)), 2)
        lax.fori_loop(first, end, one_tile, 0)

    def own_sends(phase, direction):
        for part in (2 * phase, 2 * phase + 1):
            if direction == "left":
                to_left(me, part).start()
            else:
                to_right(me, part).start()

    for part in range(4):
        for load in loads[part]:
            load.wait()
        phase = part // 2
        if phase == 0:
            @pl.when(chip > low)
            def _():
                to_left(me, part).start()

            @pl.when(chip < high)
            def _():
                to_right(me, part).start()

            @pl.when(inner)
            def _():
                to_mate(me, part).start()
        else:
            @pl.when(((chip <= low) & (chip > 0)) | (chip == last))
            def _():
                to_left(me, part).start()

            @pl.when(((chip >= high) & (chip < last)) | (chip == 0))
            def _():
                to_right(me, part).start()

            to_mate(me, part).start()

    for head in range(heads):
        tile, at = divmod(head, heads_per_tile)
        qs[tile, at * new_rows:(at + 1) * new_rows, :] = q_ref[:, head * HEAD_DIM:(head + 1) * HEAD_DIM]
    tops[...] = jnp.full_like(tops, MASKED)
    totals[...] = jnp.zeros_like(totals)
    acc[...] = jnp.zeros_like(acc)

    @pl.when(helper)
    def _():
        for slot in range(HELPED):
            q_copy(slot, me).wait_recv()
            for head in range(heads // 2):
                tile, at = divmod(head, heads_per_tile)
                qs[4 + 2 * slot + tile, at * new_rows:(at + 1) * new_rows, :] = (
                    q_in[slot, :, head * HEAD_DIM:(head + 1) * HEAD_DIM])

    def take(at_chip, first_phase, phases):
        def one(n, carry):
            block = at_chip * 2 + jnp.where(n % 2 == 0, core, 1 - core)
            phase = first_phase + n // 2

            @pl.when(goes_mate(phase))
            def _():
                @pl.when(n % 2 == 1)
                def _():
                    for part in range(2):
                        to_mate(block, 2 * phase + part).wait_recv()

                compute(block, phase)
            return carry
        lax.fori_loop(0, 2 * phases, one, 0)

    take(chip, 0, 2)

    def from_left(turn):
        late = turn - 2 * ahead
        phase = jnp.where(helped_right, 1, jnp.where(turn <= behind, 0, 1))
        step = jnp.where(helped_right, late, jnp.where(turn <= behind, turn, turn - behind))
        return (step >= 1) & (step <= behind), chip - step, phase

    def from_right(turn):
        late = turn - 2 * behind
        phase = jnp.where(helped_left, 1, jnp.where(turn <= ahead, 0, 1))
        step = jnp.where(helped_left, late, jnp.where(turn <= ahead, turn, turn - ahead))
        return (step >= 1) & (step <= ahead), chip + step, phase

    def pass_on(turn, half):
        there, at_chip, phase = from_left(turn)

        @pl.when(there)
        def _():
            block, part = at_chip * 2 + core, 2 * phase + half
            to_mate(block, part).wait_recv()

            @pl.when(goes_right(phase))
            def _():
                to_right(block, part).start()

            @pl.when(goes_mate(phase))
            def _():
                to_mate(block, part).start()

        there, at_chip, phase = from_right(turn)

        @pl.when(there)
        def _():
            block, part = at_chip * 2 + core, 2 * phase + half
            to_mate(block, part).wait_recv()

            @pl.when(goes_left(phase))
            def _():
                to_left(block, part).start()

            @pl.when(goes_mate(phase))
            def _():
                to_mate(block, part).start()

    turns = max(2 * high, chips + HELPED)
    answered = chips - HELPED

    def one_turn(turn, carry):
        pass_on(turn, 0)

        @pl.when(helper & (turn == answered + 1))
        def _():
            for slot in range(HELPED):
                o_copy(slot, helped_device(slot)).start()

        there, at_chip, phase = from_left(turn - 1)

        @pl.when(there & (turn > 1))
        def _():
            take(at_chip, phase, 1)

        pass_on(turn, 1)

        @pl.when((turn == behind) & (chip < high))
        def _():
            own_sends(1, "right")

        @pl.when((turn == ahead) & (chip > low))
        def _():
            own_sends(1, "left")

        there, at_chip, phase = from_right(turn - 1)

        @pl.when(there & (turn > 1))
        def _():
            take(at_chip, phase, 1)

        @pl.when(helper & (turn == answered))
        def _():
            for slot in range(HELPED):
                for n in range(2):
                    put(o_out.at[slot], n, 4 + 2 * slot + n)
        return carry

    def put(target, place, tile):
        result = jnp.transpose(acc[tile] / totals[tile]).astype(jnp.bfloat16)
        for at in range(heads_per_tile):
            head = place * heads_per_tile + at
            target[:, head * HEAD_DIM:(head + 1) * HEAD_DIM] = result[at * new_rows:(at + 1) * new_rows]

    lax.fori_loop(1, turns + 2, one_turn, 0)

    for n in range(2):
        put(out_ref, n, n)

    @pl.when(inner)
    def _():
        for n in range(2, 4):
            put(out_ref, n, n)

    @pl.when(helped)
    def _():
        o_copy(0, my_helper).wait_recv()
        out_ref[:, half_width:] = o_in[...]
        q_copy(my_slot, my_helper).wait_send()

    @pl.when(helper)
    def _():
        for slot in range(HELPED):
            o_copy(slot, me).wait_send()

    def finish(n, carry):
        at_chip, part = n // 4, n % 4
        phase = part // 2
        block = at_chip * 2 + core

        @pl.when(goes_left(phase) & (at_chip >= chip))
        def _():
            to_left(block, part).wait_send()

        @pl.when(goes_right(phase) & (at_chip <= chip))
        def _():
            to_right(block, part).wait_send()

        @pl.when(goes_mate(phase))
        def _():
            to_mate(block, part).wait_send()
        return carry

    lax.fori_loop(0, 4 * chips, finish, 0)


def local(queries, cache_keys, cache_values, new_keys, new_values, prefix_len):
    count = lax.axis_size("ctx")
    chips = count // 2
    rows, width = queries.shape
    key_rows = cache_keys.shape[0] + new_keys.shape[0]
    tiles = 4 + 2 * HELPED
    dma = pltpu.SemaphoreType.DMA
    anywhere = pl.BlockSpec(memory_space=pl.ANY)
    return pl.pallas_call(
        functools.partial(kernel, chips),
        out_shape=jax.ShapeDtypeStruct((rows, width), jnp.bfloat16),
        in_specs=[pl.BlockSpec(memory_space=pltpu.SMEM), pl.BlockSpec(memory_space=pltpu.VMEM)] + [anywhere] * 4,
        out_specs=pl.BlockSpec(memory_space=pltpu.VMEM),
        scratch_shapes=[
            pltpu.VMEM((count, 4, key_rows, HEAD_DIM), jnp.bfloat16),
            pltpu.VMEM((tiles, TILE, HEAD_DIM), jnp.bfloat16),
            pltpu.VMEM((tiles, 1, TILE), jnp.float32),
            pltpu.VMEM((tiles, 1, TILE), jnp.float32),
            pltpu.VMEM((tiles, HEAD_DIM, TILE), jnp.float32),
            pltpu.VMEM((HELPED, rows, width // 2), jnp.bfloat16),
            pltpu.VMEM((rows, width // 2), jnp.bfloat16),
            pltpu.VMEM((HELPED, rows, width // 2), jnp.bfloat16),
            dma((8,)), dma((chips, 4)), dma((chips, 4)), dma((chips, 4)), dma((count, 4)),
            dma((1,)), dma((HELPED,)), dma((HELPED,)), dma((1,)),
        ],
        compiler_params=pltpu.CompilerParams(collective_id=0, has_side_effects=True),
    )(prefix_len, queries, cache_keys, cache_values, new_keys, new_values)


def solution(mesh):
    spec = P(("dp", "ctx"), "tp")
    return jax.shard_map(
        local, mesh=mesh, in_specs=(spec,) * 5 + (P("dp"),), out_specs=spec, check_vma=False)
```

```python
import functools

import jax
import jax.numpy as jnp
from jax import lax
from jax.experimental import pallas as pl
from jax.experimental.pallas import tpu as pltpu
from jax.sharding import PartitionSpec as P

HEAD_DIM = 128
LOG2_E = 1.4426950408889634
MASKED = -1e30
TILE = 256


HELPED = 1


def kernel(chips, length_ref, q_ref, ck_ref, cv_ref, nk_ref, nv_ref, out_ref,
           held, qs, tops, totals, acc, q_in, o_in, o_out,
           local_sem, left_sem, right_sem, mate_sem, recv_sem, q_sems, o_sems, q_recv, o_recv):
    me = lax.axis_index("ctx")
    chip = me // 2
    core = me % 2
    last = chips - 1
    low, high = HELPED, last - HELPED
    inner = (chip >= low) & (chip <= high)
    helper = (chip == low) | (chip == high)
    helped_left, helped_right = chip < low, chip > high
    helped = helped_left | helped_right
    behind, ahead = chip, last - chip
    cache_rows = ck_ref.shape[0]
    new_rows = nk_ref.shape[0]
    key_rows = cache_rows + new_rows
    heads = q_ref.shape[1] // HEAD_DIM
    heads_per_tile = TILE // new_rows
    half_width = q_ref.shape[1] // 2
    length = length_ref[0]
    scale = (HEAD_DIM ** -0.5) * LOG2_E
    mate = chip * 2 + 1 - core
    my_helper = jnp.where(helped_left, low, high) * 2 + core
    my_slot = jnp.where(helped_left, chip, last - chip)

    def helped_device(slot):
        return jnp.where(chip == low, slot, last - slot) * 2 + core

    loads = []
    for part in range(4):
        cached, fresh = ((ck_ref, nk_ref), (cv_ref, nv_ref))[part % 2]
        cols = pl.ds((1 - part // 2) * HEAD_DIM, HEAD_DIM)
        pair = (
            pltpu.make_async_copy(
                cached.at[:, cols], held.at[me, part, pl.ds(0, cache_rows)], local_sem.at[2 * part]),
            pltpu.make_async_copy(
                fresh.at[:, cols], held.at[me, part, pl.ds(cache_rows, new_rows)], local_sem.at[2 * part + 1]),
        )
        for load in pair:
            load.start()
        loads.append(pair)

    barrier = pltpu.get_barrier_semaphore()

    def greet(device):
        pl.semaphore_signal(barrier, inc=1, device_id={"ctx": device})

    greet(mate)

    @pl.when(chip > 0)
    def _():
        greet(me - 2)

    @pl.when(chip < last)
    def _():
        greet(me + 2)

    far = helped & (my_slot < HELPED - 1)

    @pl.when(far)
    def _():
        greet(my_helper)

    @pl.when(helper)
    def _():
        for slot in range(HELPED - 1):
            greet(helped_device(slot))

    def as_int(flag):
        return flag.astype(jnp.int32)

    pl.semaphore_wait(
        barrier,
        1 + as_int(chip > 0) + as_int(chip < last) + as_int(far) + as_int(helper) * (HELPED - 1))

    def q_copy(slot, device):
        return pltpu.make_async_remote_copy(
            src_ref=q_ref.at[:, pl.ds(half_width, half_width)], dst_ref=q_in.at[slot],
            send_sem=q_sems.at[0], recv_sem=q_recv.at[slot], device_id={"ctx": device})

    def o_copy(slot, device):
        return pltpu.make_async_remote_copy(
            src_ref=o_out.at[slot], dst_ref=o_in, send_sem=o_sems.at[slot],
            recv_sem=o_recv.at[0], device_id={"ctx": device})

    @pl.when(helped)
    def _():
        q_copy(my_slot, my_helper).start()

    def copy_of(block, part, sems, target):
        piece = held.at[block, part]
        return pltpu.make_async_remote_copy(
            src_ref=piece, dst_ref=piece, send_sem=sems.at[block // 2, part],
            recv_sem=recv_sem.at[block, part], device_id={"ctx": target})

    def to_left(block, part):
        return copy_of(block, part, left_sem, me - 2)

    def to_right(block, part):
        return copy_of(block, part, right_sem, me + 2)

    def to_mate(block, part):
        return copy_of(block, part, mate_sem, mate)

    def goes_left(phase):
        return jnp.where(phase == 0, chip > low, chip > 0)

    def goes_right(phase):
        return jnp.where(phase == 0, chip < high, chip < last)

    def goes_mate(phase):
        return inner | (phase == 1)

    def compute(block, phase):
        def one_tile(n, carry):
            keys = held[block, 2 * phase]
            values = held[block, 2 * phase + 1]
            asker = jnp.where(n < 4, me, helped_device((n - 4) // 2))
            scores = lax.dot_general(
                keys, qs[n], (((1,), (1,)), ((), ())),
                preferred_element_type=jnp.float32) * scale
            row = lax.broadcasted_iota(jnp.int32, (cache_rows, TILE), 0)
            cached = jnp.where(row + block * cache_rows < length, scores[:cache_rows], MASKED)
            new_row = lax.broadcasted_iota(jnp.int32, (new_rows, TILE), 0)
            token = lax.broadcasted_iota(jnp.int32, (new_rows, TILE), 1) % new_rows
            fresh = jnp.where(
                new_row + block * new_rows <= token + asker * new_rows, scores[cache_rows:], MASKED)
            old_top = tops[n]
            top = jnp.maximum(jnp.max(cached, 0, keepdims=True), jnp.max(fresh, 0, keepdims=True))
            top = jnp.maximum(old_top, top)
            weights = jnp.exp2(jnp.concatenate([cached, fresh], 0) - top)
            rescale = jnp.exp2(old_top - top)
            tops[n] = top
            totals[n] = totals[n] * rescale + jnp.sum(weights, 0, keepdims=True)
            acc[n] = acc[n] * rescale + lax.dot_general(
                values, weights.astype(jnp.bfloat16), (((0,), (0,)), ((), ())),
                preferred_element_type=jnp.float32)
            return carry

        first = jnp.where(phase == 0, 2, 0)
        end = jnp.where(phase == 0, jnp.where(helper, 4 + 2 * HELPED, jnp.where(inner, 4, 2)), 2)
        lax.fori_loop(first, end, one_tile, 0)

    def own_sends(phase, direction):
        for part in (2 * phase, 2 * phase + 1):
            if direction == "left":
                to_left(me, part).start()
            else:
                to_right(me, part).start()

    for part in range(4):
        for load in loads[part]:
            load.wait()
        phase = part // 2
        if phase == 0:
            @pl.when(chip > low)
            def _():
                to_left(me, part).start()

            @pl.when(chip < high)
            def _():
                to_right(me, part).start()

            @pl.when(inner)
            def _():
                to_mate(me, part).start()
        else:
            @pl.when(((chip <= low) & (chip > 0)) | (chip == last))
            def _():
                to_left(me, part).start()

            @pl.when(((chip >= high) & (chip < last)) | (chip == 0))
            def _():
                to_right(me, part).start()

            to_mate(me, part).start()

    for head in range(heads):
        tile, at = divmod(head, heads_per_tile)
        qs[tile, at * new_rows:(at + 1) * new_rows, :] = q_ref[:, head * HEAD_DIM:(head + 1) * HEAD_DIM]
    tops[...] = jnp.full_like(tops, MASKED)
    totals[...] = jnp.zeros_like(totals)
    acc[...] = jnp.zeros_like(acc)

    @pl.when(helper)
    def _():
        for slot in range(HELPED):
            q_copy(slot, me).wait_recv()
            for head in range(heads // 2):
                tile, at = divmod(head, heads_per_tile)
                qs[4 + 2 * slot + tile, at * new_rows:(at + 1) * new_rows, :] = (
                    q_in[slot, :, head * HEAD_DIM:(head + 1) * HEAD_DIM])

    def take(at_chip, first_phase, phases):
        def one(n, carry):
            block = at_chip * 2 + jnp.where(n % 2 == 0, core, 1 - core)
            phase = first_phase + n // 2

            @pl.when(goes_mate(phase))
            def _():
                @pl.when(n % 2 == 1)
                def _():
                    for part in range(2):
                        to_mate(block, 2 * phase + part).wait_recv()

                compute(block, phase)
            return carry
        lax.fori_loop(0, 2 * phases, one, 0)

    take(chip, 0, 2)

    def from_left(turn):
        late = turn - 2 * ahead
        phase = jnp.where(helped_right, 1, jnp.where(turn <= behind, 0, 1))
        step = jnp.where(helped_right, late, jnp.where(turn <= behind, turn, turn - behind))
        return (step >= 1) & (step <= behind), chip - step, phase

    def from_right(turn):
        late = turn - 2 * behind
        phase = jnp.where(helped_left, 1, jnp.where(turn <= ahead, 0, 1))
        step = jnp.where(helped_left, late, jnp.where(turn <= ahead, turn, turn - ahead))
        return (step >= 1) & (step <= ahead), chip + step, phase

    def pass_on(turn, half):
        there, at_chip, phase = from_left(turn)

        @pl.when(there)
        def _():
            block, part = at_chip * 2 + core, 2 * phase + half
            to_mate(block, part).wait_recv()

            @pl.when(goes_right(phase))
            def _():
                to_right(block, part).start()

            @pl.when(goes_mate(phase))
            def _():
                to_mate(block, part).start()

        there, at_chip, phase = from_right(turn)

        @pl.when(there)
        def _():
            block, part = at_chip * 2 + core, 2 * phase + half
            to_mate(block, part).wait_recv()

            @pl.when(goes_left(phase))
            def _():
                to_left(block, part).start()

            @pl.when(goes_mate(phase))
            def _():
                to_mate(block, part).start()

    turns = max(2 * high, chips + HELPED)
    answered = chips - HELPED

    def one_turn(turn, carry):
        pass_on(turn, 0)

        @pl.when(helper & (turn == answered + 1))
        def _():
            for slot in range(HELPED):
                o_copy(slot, helped_device(slot)).start()

        there, at_chip, phase = from_left(turn - 1)

        @pl.when(there & (turn > 1))
        def _():
            take(at_chip, phase, 1)

        pass_on(turn, 1)

        @pl.when((turn == behind) & (chip < high))
        def _():
            own_sends(1, "right")

        @pl.when((turn == ahead) & (chip > low))
        def _():
            own_sends(1, "left")

        there, at_chip, phase = from_right(turn - 1)

        @pl.when(there & (turn > 1))
        def _():
            take(at_chip, phase, 1)

        @pl.when(helper & (turn == answered))
        def _():
            for slot in range(HELPED):
                for n in range(2):
                    put(o_out.at[slot], n, 4 + 2 * slot + n)
        return carry

    def put(target, place, tile):
        result = jnp.transpose(acc[tile] / totals[tile]).astype(jnp.bfloat16)
        for at in range(heads_per_tile):
            head = place * heads_per_tile + at
            target[:, head * HEAD_DIM:(head + 1) * HEAD_DIM] = result[at * new_rows:(at + 1) * new_rows]

    lax.fori_loop(1, turns + 2, one_turn, 0)

    for n in range(2):
        put(out_ref, n, n)

    @pl.when(inner)
    def _():
        for n in range(2, 4):
            put(out_ref, n, n)

    @pl.when(helped)
    def _():
        o_copy(0, my_helper).wait_recv()
        out_ref[:, half_width:] = o_in[...]
        q_copy(my_slot, my_helper).wait_send()

    @pl.when(helper)
    def _():
        for slot in range(HELPED):
            o_copy(slot, me).wait_send()

    def finish(n, carry):
        at_chip, part = n // 4, n % 4
        phase = part // 2
        block = at_chip * 2 + core

        @pl.when(goes_left(phase) & (at_chip >= chip))
        def _():
            to_left(block, part).wait_send()

        @pl.when(goes_right(phase) & (at_chip <= chip))
        def _():
            to_right(block, part).wait_send()

        @pl.when(goes_mate(phase))
        def _():
            to_mate(block, part).wait_send()
        return carry

    lax.fori_loop(0, 4 * chips, finish, 0)


def local(queries, cache_keys, cache_values, new_keys, new_values, prefix_len):
    count = lax.axis_size("ctx")
    chips = count // 2
    rows, width = queries.shape
    key_rows = cache_keys.shape[0] + new_keys.shape[0]
    tiles = 4 + 2 * HELPED
    dma = pltpu.SemaphoreType.DMA
    anywhere = pl.BlockSpec(memory_space=pl.ANY)
    return pl.pallas_call(
        functools.partial(kernel, chips),
        out_shape=jax.ShapeDtypeStruct((rows, width), jnp.bfloat16),
        in_specs=[pl.BlockSpec(memory_space=pltpu.SMEM), pl.BlockSpec(memory_space=pltpu.VMEM)] + [anywhere] * 4,
        out_specs=pl.BlockSpec(memory_space=pltpu.VMEM),
        scratch_shapes=[
            pltpu.VMEM((count, 4, key_rows, HEAD_DIM), jnp.bfloat16),
            pltpu.VMEM((tiles, TILE, HEAD_DIM), jnp.bfloat16),
            pltpu.VMEM((tiles, 1, TILE), jnp.float32),
            pltpu.VMEM((tiles, 1, TILE), jnp.float32),
            pltpu.VMEM((tiles, HEAD_DIM, TILE), jnp.float32),
            pltpu.VMEM((HELPED, rows, width // 2), jnp.bfloat16),
            pltpu.VMEM((rows, width // 2), jnp.bfloat16),
            pltpu.VMEM((HELPED, rows, width // 2), jnp.bfloat16),
            dma((8,)), dma((chips, 4)), dma((chips, 4)), dma((chips, 4)), dma((count, 4)),
            dma((1,)), dma((HELPED,)), dma((HELPED,)), dma((1,)),
        ],
        compiler_params=pltpu.CompilerParams(collective_id=0, has_side_effects=True),
    )(prefix_len, queries, cache_keys, cache_values, new_keys, new_values)


def solution(mesh):
    spec = P(("dp", "ctx"), "tp")
    return jax.shard_map(
        local, mesh=mesh, in_specs=(spec,) * 5 + (P("dp"),), out_specs=spec, check_vma=False)
```

```python
import functools

import jax
import jax.numpy as jnp
from jax import lax
from jax.experimental import pallas as pl
from jax.experimental.pallas import tpu as pltpu
from jax.sharding import PartitionSpec as P

HEAD_DIM = 128
LOG2_E = 1.4426950408889634
MASKED = -1e30
TILE = 256


HELPED = 1


def kernel(chips, length_ref, q_ref, ck_ref, cv_ref, nk_ref, nv_ref, out_ref,
           held, qs, tops, totals, acc, q_in, o_in, o_out,
           local_sem, left_sem, right_sem, mate_sem, recv_sem, q_sems, o_sems, q_recv, o_recv):
    me = lax.axis_index("ctx")
    chip = me // 2
    core = me % 2
    last = chips - 1
    low, high = HELPED, last - HELPED
    inner = (chip >= low) & (chip <= high)
    helper = (chip == low) | (chip == high)
    helped_left, helped_right = chip < low, chip > high
    helped = helped_left | helped_right
    behind, ahead = chip, last - chip
    cache_rows = ck_ref.shape[0]
    new_rows = nk_ref.shape[0]
    key_rows = cache_rows + new_rows
    heads = q_ref.shape[1] // HEAD_DIM
    heads_per_tile = TILE // new_rows
    half_width = q_ref.shape[1] // 2
    length = length_ref[0]
    scale = (HEAD_DIM ** -0.5) * LOG2_E
    mate = chip * 2 + 1 - core
    my_helper = jnp.where(helped_left, low, high) * 2 + core
    my_slot = jnp.where(helped_left, chip, last - chip)

    def helped_device(slot):
        return jnp.where(chip == low, slot, last - slot) * 2 + core

    loads = []
    for part in range(4):
        cached, fresh = ((ck_ref, nk_ref), (cv_ref, nv_ref))[part % 2]
        cols = pl.ds((1 - part // 2) * HEAD_DIM, HEAD_DIM)
        pair = (
            pltpu.make_async_copy(
                cached.at[:, cols], held.at[me, part, pl.ds(0, cache_rows)], local_sem.at[2 * part]),
            pltpu.make_async_copy(
                fresh.at[:, cols], held.at[me, part, pl.ds(cache_rows, new_rows)], local_sem.at[2 * part + 1]),
        )
        for load in pair:
            load.start()
        loads.append(pair)

    barrier = pltpu.get_barrier_semaphore()

    def greet(device):
        pl.semaphore_signal(barrier, inc=1, device_id={"ctx": device})

    greet(mate)

    @pl.when(chip > 0)
    def _():
        greet(me - 2)

    @pl.when(chip < last)
    def _():
        greet(me + 2)

    far = helped & (my_slot < HELPED - 1)

    @pl.when(far)
    def _():
        greet(my_helper)

    @pl.when(helper)
    def _():
        for slot in range(HELPED - 1):
            greet(helped_device(slot))

    def as_int(flag):
        return flag.astype(jnp.int32)

    pl.semaphore_wait(
        barrier,
        1 + as_int(chip > 0) + as_int(chip < last) + as_int(far) + as_int(helper) * (HELPED - 1))

    def q_copy(slot, device):
        return pltpu.make_async_remote_copy(
            src_ref=q_ref.at[:, pl.ds(half_width, half_width)], dst_ref=q_in.at[slot],
            send_sem=q_sems.at[0], recv_sem=q_recv.at[slot], device_id={"ctx": device})

    def o_copy(slot, device):
        return pltpu.make_async_remote_copy(
            src_ref=o_out.at[slot], dst_ref=o_in, send_sem=o_sems.at[slot],
            recv_sem=o_recv.at[0], device_id={"ctx": device})

    @pl.when(helped)
    def _():
        q_copy(my_slot, my_helper).start()

    def copy_of(block, part, sems, target):
        piece = held.at[block, part]
        return pltpu.make_async_remote_copy(
            src_ref=piece, dst_ref=piece, send_sem=sems.at[block // 2, part],
            recv_sem=recv_sem.at[block, part], device_id={"ctx": target})

    def to_left(block, part):
        return copy_of(block, part, left_sem, me - 2)

    def to_right(block, part):
        return copy_of(block, part, right_sem, me + 2)

    def to_mate(block, part):
        return copy_of(block, part, mate_sem, mate)

    def goes_left(phase):
        return jnp.where(phase == 0, chip > low, chip > 0)

    def goes_right(phase):
        return jnp.where(phase == 0, chip < high, chip < last)

    def goes_mate(phase):
        return inner | (phase == 1)

    def compute(block, phase):
        def one_pair(pair, carry):
            keys = held[block, 2 * phase]
            values = held[block, 2 * phase + 1]
            asker = jnp.where(pair < 2, me, helped_device(pair - 2))
            both = [2 * pair, 2 * pair + 1]
            asked = [qs[n] for n in both]
            old_tops = [tops[n] for n in both]
            old_totals = [totals[n] for n in both]
            old_acc = [acc[n] for n in both]
            limit = length - block * cache_rows
            ahead_by = (block - asker) * new_rows
            row = lax.broadcasted_iota(jnp.int32, (cache_rows, TILE), 0)
            new_row = lax.broadcasted_iota(jnp.int32, (new_rows, TILE), 0)
            token = lax.broadcasted_iota(jnp.int32, (new_rows, TILE), 1) % new_rows
            stored = row < limit
            seen = new_row - token <= -ahead_by
            scores = [
                lax.dot_general(keys, q, (((1,), (1,)), ((), ())), preferred_element_type=jnp.float32) * scale
                for q in asked]
            results = []
            for n in range(2):
                cached = jnp.where(stored, scores[n][:cache_rows], MASKED)
                fresh = jnp.where(seen, scores[n][cache_rows:], MASKED)
                top = jnp.maximum(jnp.max(cached, 0, keepdims=True), jnp.max(fresh, 0, keepdims=True))
                top = jnp.maximum(old_tops[n], top)
                weights = jnp.exp2(jnp.concatenate([cached, fresh], 0) - top)
                rescale = jnp.exp2(old_tops[n] - top)
                total = old_totals[n] * rescale + jnp.sum(weights, 0, keepdims=True)
                part = lax.dot_general(
                    values, weights.astype(jnp.bfloat16), (((0,), (0,)), ((), ())),
                    preferred_element_type=jnp.float32)
                results.append((top, total, old_acc[n] * rescale + part))
            for n, (top, total, summed) in zip(both, results):
                tops[n] = top
                totals[n] = total
                acc[n] = summed
            return carry

        first = jnp.where(phase == 0, 1, 0)
        end = jnp.where(phase == 0, jnp.where(helper, 2 + HELPED, jnp.where(inner, 2, 1)), 1)
        lax.fori_loop(first, end, one_pair, 0)

    def own_sends(phase, direction):
        for part in (2 * phase, 2 * phase + 1):
            if direction == "left":
                to_left(me, part).start()
            else:
                to_right(me, part).start()

    for part in range(4):
        for load in loads[part]:
            load.wait()
        phase = part // 2
        if phase == 0:
            @pl.when(chip > low)
            def _():
                to_left(me, part).start()

            @pl.when(chip < high)
            def _():
                to_right(me, part).start()

            @pl.when(inner)
            def _():
                to_mate(me, part).start()
        else:
            @pl.when(((chip <= low) & (chip > 0)) | (chip == last))
            def _():
                to_left(me, part).start()

            @pl.when(((chip >= high) & (chip < last)) | (chip == 0))
            def _():
                to_right(me, part).start()

            to_mate(me, part).start()

    for head in range(heads):
        tile, at = divmod(head, heads_per_tile)
        qs[tile, at * new_rows:(at + 1) * new_rows, :] = q_ref[:, head * HEAD_DIM:(head + 1) * HEAD_DIM]
    tops[...] = jnp.full_like(tops, MASKED)
    totals[...] = jnp.zeros_like(totals)
    acc[...] = jnp.zeros_like(acc)

    @pl.when(helper)
    def _():
        for slot in range(HELPED):
            q_copy(slot, me).wait_recv()
            for head in range(heads // 2):
                tile, at = divmod(head, heads_per_tile)
                qs[4 + 2 * slot + tile, at * new_rows:(at + 1) * new_rows, :] = (
                    q_in[slot, :, head * HEAD_DIM:(head + 1) * HEAD_DIM])

    def take(at_chip, first_phase, phases):
        def one(n, carry):
            block = at_chip * 2 + jnp.where(n % 2 == 0, core, 1 - core)
            phase = first_phase + n // 2

            @pl.when(goes_mate(phase))
            def _():
                @pl.when(n % 2 == 1)
                def _():
                    for part in range(2):
                        to_mate(block, 2 * phase + part).wait_recv()

                compute(block, phase)
            return carry
        lax.fori_loop(0, 2 * phases, one, 0)

    take(chip, 0, 2)

    def from_left(turn):
        late = turn - 2 * ahead
        phase = jnp.where(helped_right, 1, jnp.where(turn <= behind, 0, 1))
        step = jnp.where(helped_right, late, jnp.where(turn <= behind, turn, turn - behind))
        return (step >= 1) & (step <= behind), chip - step, phase

    def from_right(turn):
        late = turn - 2 * behind
        phase = jnp.where(helped_left, 1, jnp.where(turn <= ahead, 0, 1))
        step = jnp.where(helped_left, late, jnp.where(turn <= ahead, turn, turn - ahead))
        return (step >= 1) & (step <= ahead), chip + step, phase

    def pass_on(turn, half):
        there, at_chip, phase = from_left(turn)

        @pl.when(there)
        def _():
            block, part = at_chip * 2 + core, 2 * phase + half
            to_mate(block, part).wait_recv()

            @pl.when(goes_right(phase))
            def _():
                to_right(block, part).start()

            @pl.when(goes_mate(phase))
            def _():
                to_mate(block, part).start()

        there, at_chip, phase = from_right(turn)

        @pl.when(there)
        def _():
            block, part = at_chip * 2 + core, 2 * phase + half
            to_mate(block, part).wait_recv()

            @pl.when(goes_left(phase))
            def _():
                to_left(block, part).start()

            @pl.when(goes_mate(phase))
            def _():
                to_mate(block, part).start()

    turns = max(2 * high, chips + HELPED)
    answered = chips - HELPED

    def one_turn(turn, carry):
        pass_on(turn, 0)

        @pl.when(helper & (turn == answered + 1))
        def _():
            for slot in range(HELPED):
                o_copy(slot, helped_device(slot)).start()

        there, at_chip, phase = from_left(turn - 1)

        @pl.when(there & (turn > 1))
        def _():
            take(at_chip, phase, 1)

        pass_on(turn, 1)

        @pl.when((turn == behind) & (chip < high))
        def _():
            own_sends(1, "right")

        @pl.when((turn == ahead) & (chip > low))
        def _():
            own_sends(1, "left")

        there, at_chip, phase = from_right(turn - 1)

        @pl.when(there & (turn > 1))
        def _():
            take(at_chip, phase, 1)

        @pl.when(helper & (turn == answered))
        def _():
            for slot in range(HELPED):
                for n in range(2):
                    put(o_out.at[slot], n, 4 + 2 * slot + n)
        return carry

    def put(target, place, tile):
        result = jnp.transpose(acc[tile] / totals[tile]).astype(jnp.bfloat16)
        for at in range(heads_per_tile):
            head = place * heads_per_tile + at
            target[:, head * HEAD_DIM:(head + 1) * HEAD_DIM] = result[at * new_rows:(at + 1) * new_rows]

    lax.fori_loop(1, turns + 2, one_turn, 0)

    for n in range(2):
        put(out_ref, n, n)

    @pl.when(inner)
    def _():
        for n in range(2, 4):
            put(out_ref, n, n)

    @pl.when(helped)
    def _():
        o_copy(0, my_helper).wait_recv()
        out_ref[:, half_width:] = o_in[...]
        q_copy(my_slot, my_helper).wait_send()

    @pl.when(helper)
    def _():
        for slot in range(HELPED):
            o_copy(slot, me).wait_send()

    def finish(n, carry):
        at_chip, part = n // 4, n % 4
        phase = part // 2
        block = at_chip * 2 + core

        @pl.when(goes_left(phase) & (at_chip >= chip))
        def _():
            to_left(block, part).wait_send()

        @pl.when(goes_right(phase) & (at_chip <= chip))
        def _():
            to_right(block, part).wait_send()

        @pl.when(goes_mate(phase))
        def _():
            to_mate(block, part).wait_send()
        return carry

    lax.fori_loop(0, 4 * chips, finish, 0)


def local(queries, cache_keys, cache_values, new_keys, new_values, prefix_len):
    count = lax.axis_size("ctx")
    chips = count // 2
    rows, width = queries.shape
    key_rows = cache_keys.shape[0] + new_keys.shape[0]
    tiles = 4 + 2 * HELPED
    dma = pltpu.SemaphoreType.DMA
    anywhere = pl.BlockSpec(memory_space=pl.ANY)
    return pl.pallas_call(
        functools.partial(kernel, chips),
        out_shape=jax.ShapeDtypeStruct((rows, width), jnp.bfloat16),
        in_specs=[pl.BlockSpec(memory_space=pltpu.SMEM), pl.BlockSpec(memory_space=pltpu.VMEM)] + [anywhere] * 4,
        out_specs=pl.BlockSpec(memory_space=pltpu.VMEM),
        scratch_shapes=[
            pltpu.VMEM((count, 4, key_rows, HEAD_DIM), jnp.bfloat16),
            pltpu.VMEM((tiles, TILE, HEAD_DIM), jnp.bfloat16),
            pltpu.VMEM((tiles, 1, TILE), jnp.float32),
            pltpu.VMEM((tiles, 1, TILE), jnp.float32),
            pltpu.VMEM((tiles, HEAD_DIM, TILE), jnp.float32),
            pltpu.VMEM((HELPED, rows, width // 2), jnp.bfloat16),
            pltpu.VMEM((rows, width // 2), jnp.bfloat16),
            pltpu.VMEM((HELPED, rows, width // 2), jnp.bfloat16),
            dma((8,)), dma((chips, 4)), dma((chips, 4)), dma((chips, 4)), dma((count, 4)),
            dma((1,)), dma((HELPED,)), dma((HELPED,)), dma((1,)),
        ],
        compiler_params=pltpu.CompilerParams(collective_id=0, has_side_effects=True),
    )(prefix_len, queries, cache_keys, cache_values, new_keys, new_values)


def solution(mesh):
    spec = P(("dp", "ctx"), "tp")
    return jax.shard_map(
        local, mesh=mesh, in_specs=(spec,) * 5 + (P("dp"),), out_specs=spec, check_vma=False)
```

```python
import functools

import jax
import jax.numpy as jnp
from jax import lax
from jax.experimental import pallas as pl
from jax.experimental.pallas import tpu as pltpu
from jax.sharding import PartitionSpec as P

HEAD_DIM = 128
LOG2_E = 1.4426950408889634
MASKED = -1e30
TILE = 256


HELPED = 2


def kernel(chips, length_ref, q_ref, ck_ref, cv_ref, nk_ref, nv_ref, out_ref,
           held, qs, tops, totals, acc, q_in, o_in, o_out,
           local_sem, left_sem, right_sem, mate_sem, recv_sem, q_sems, o_sems):
    me = lax.axis_index("ctx")
    chip = me // 2
    core = me % 2
    last = chips - 1
    low, high = HELPED, last - HELPED
    inner = (chip >= low) & (chip <= high)
    helper = inner & ((chip < low + HELPED) | (chip > high - HELPED))
    helped_left, helped_right = chip < low, chip > high
    helped = helped_left | helped_right
    behind, ahead = chip, last - chip
    cache_rows = ck_ref.shape[0]
    new_rows = nk_ref.shape[0]
    key_rows = cache_rows + new_rows
    heads = q_ref.shape[1] // HEAD_DIM
    heads_per_tile = TILE // new_rows
    half_width = q_ref.shape[1] // 2
    length = length_ref[0]
    scale = (HEAD_DIM ** -0.5) * LOG2_E
    mate = chip * 2 + 1 - core
    lower = chip < chips // 2
    partner = me + jnp.where(lower == helped, 2 * HELPED, -2 * HELPED)

    loads = []
    for part in range(4):
        cached, fresh = ((ck_ref, nk_ref), (cv_ref, nv_ref))[part % 2]
        cols = pl.ds((1 - part // 2) * HEAD_DIM, HEAD_DIM)
        pair = (
            pltpu.make_async_copy(
                cached.at[:, cols], held.at[me, part, pl.ds(0, cache_rows)], local_sem.at[2 * part]),
            pltpu.make_async_copy(
                fresh.at[:, cols], held.at[me, part, pl.ds(cache_rows, new_rows)], local_sem.at[2 * part + 1]),
        )
        for load in pair:
            load.start()
        loads.append(pair)

    barrier = pltpu.get_barrier_semaphore()

    def greet(device):
        pl.semaphore_signal(barrier, inc=1, device_id={"ctx": device})

    greet(mate)

    @pl.when(chip > 0)
    def _():
        greet(me - 2)

    @pl.when(chip < last)
    def _():
        greet(me + 2)

    far = (helped | helper) & (HELPED > 1)

    @pl.when(far)
    def _():
        greet(partner)

    def as_int(flag):
        return flag.astype(jnp.int32)

    pl.semaphore_wait(
        barrier,
        1 + as_int(chip > 0) + as_int(chip < last) + as_int(far))

    q_copy = pltpu.make_async_remote_copy(
        src_ref=q_ref.at[:, pl.ds(half_width, half_width)], dst_ref=q_in,
        send_sem=q_sems.at[0], recv_sem=q_sems.at[1], device_id={"ctx": partner})
    o_copy = pltpu.make_async_remote_copy(
        src_ref=o_out, dst_ref=o_in,
        send_sem=o_sems.at[0], recv_sem=o_sems.at[1], device_id={"ctx": partner})

    @pl.when(helped)
    def _():
        q_copy.start()

    def copy_of(block, part, sems, target):
        piece = held.at[block, part]
        return pltpu.make_async_remote_copy(
            src_ref=piece, dst_ref=piece, send_sem=sems.at[block // 2, part],
            recv_sem=recv_sem.at[block, part], device_id={"ctx": target})

    def to_left(block, part):
        return copy_of(block, part, left_sem, me - 2)

    def to_right(block, part):
        return copy_of(block, part, right_sem, me + 2)

    def to_mate(block, part):
        return copy_of(block, part, mate_sem, mate)

    def goes_left(phase):
        return jnp.where(phase == 0, chip > low, chip > 0)

    def goes_right(phase):
        return jnp.where(phase == 0, chip < high, chip < last)

    def goes_mate(phase):
        return inner | (phase == 1)

    def compute(block, phase):
        def one_pair(pair, carry):
            keys = held[block, 2 * phase]
            values = held[block, 2 * phase + 1]
            asker = jnp.where(pair < 2, me, partner)
            both = [2 * pair, 2 * pair + 1]
            asked = [qs[n] for n in both]
            old_tops = [tops[n] for n in both]
            old_totals = [totals[n] for n in both]
            old_acc = [acc[n] for n in both]
            limit = length - block * cache_rows
            ahead_by = (block - asker) * new_rows
            row = lax.broadcasted_iota(jnp.int32, (cache_rows, TILE), 0)
            new_row = lax.broadcasted_iota(jnp.int32, (new_rows, TILE), 0)
            token = lax.broadcasted_iota(jnp.int32, (new_rows, TILE), 1) % new_rows
            stored = row < limit
            seen = new_row - token <= -ahead_by
            scores = [
                lax.dot_general(keys, q, (((1,), (1,)), ((), ())), preferred_element_type=jnp.float32) * scale
                for q in asked]
            results = []
            for n in range(2):
                cached = jnp.where(stored, scores[n][:cache_rows], MASKED)
                fresh = jnp.where(seen, scores[n][cache_rows:], MASKED)
                top = jnp.maximum(jnp.max(cached, 0, keepdims=True), jnp.max(fresh, 0, keepdims=True))
                top = jnp.maximum(old_tops[n], top)
                weights = jnp.exp2(jnp.concatenate([cached, fresh], 0) - top)
                rescale = jnp.exp2(old_tops[n] - top)
                total = old_totals[n] * rescale + jnp.sum(weights, 0, keepdims=True)
                part = lax.dot_general(
                    values, weights.astype(jnp.bfloat16), (((0,), (0,)), ((), ())),
                    preferred_element_type=jnp.float32)
                results.append((top, total, old_acc[n] * rescale + part))
            for n, (top, total, summed) in zip(both, results):
                tops[n] = top
                totals[n] = total
                acc[n] = summed
            return carry

        first = jnp.where(phase == 0, 1, 0)
        end = jnp.where(phase == 0, jnp.where(helper, 3, jnp.where(inner, 2, 1)), 1)
        lax.fori_loop(first, end, one_pair, 0)

    def own_sends(phase, direction):
        for part in (2 * phase, 2 * phase + 1):
            if direction == "left":
                to_left(me, part).start()
            else:
                to_right(me, part).start()

    for part in range(4):
        for load in loads[part]:
            load.wait()
        phase = part // 2
        if phase == 0:
            @pl.when(chip > low)
            def _():
                to_left(me, part).start()

            @pl.when(chip < high)
            def _():
                to_right(me, part).start()

            @pl.when(inner)
            def _():
                to_mate(me, part).start()
        else:
            @pl.when(((chip <= low) & (chip > 0)) | (chip == last))
            def _():
                to_left(me, part).start()

            @pl.when(((chip >= high) & (chip < last)) | (chip == 0))
            def _():
                to_right(me, part).start()

            to_mate(me, part).start()

    for head in range(heads):
        tile, at = divmod(head, heads_per_tile)
        qs[tile, at * new_rows:(at + 1) * new_rows, :] = q_ref[:, head * HEAD_DIM:(head + 1) * HEAD_DIM]
    tops[...] = jnp.full_like(tops, MASKED)
    totals[...] = jnp.zeros_like(totals)
    acc[...] = jnp.zeros_like(acc)

    @pl.when(helper)
    def _():
        q_copy.wait_recv()
        for head in range(heads // 2):
            tile, at = divmod(head, heads_per_tile)
            qs[4 + tile, at * new_rows:(at + 1) * new_rows, :] = q_in[:, head * HEAD_DIM:(head + 1) * HEAD_DIM]

    def take(at_chip, first_phase, phases):
        def one(n, carry):
            block = at_chip * 2 + jnp.where(n % 2 == 0, core, 1 - core)
            phase = first_phase + n // 2

            @pl.when(goes_mate(phase))
            def _():
                @pl.when(n % 2 == 1)
                def _():
                    for part in range(2):
                        to_mate(block, 2 * phase + part).wait_recv()

                compute(block, phase)
            return carry
        lax.fori_loop(0, 2 * phases, one, 0)

    take(chip, 0, 2)

    def from_left(turn):
        late = turn - 2 * ahead
        phase = jnp.where(helped_right, 1, jnp.where(turn <= behind, 0, 1))
        step = jnp.where(helped_right, late, jnp.where(turn <= behind, turn, turn - behind))
        return (step >= 1) & (step <= behind), chip - step, phase

    def from_right(turn):
        late = turn - 2 * behind
        phase = jnp.where(helped_left, 1, jnp.where(turn <= ahead, 0, 1))
        step = jnp.where(helped_left, late, jnp.where(turn <= ahead, turn, turn - ahead))
        return (step >= 1) & (step <= ahead), chip + step, phase

    def pass_on(turn, half):
        there, at_chip, phase = from_left(turn)

        @pl.when(there)
        def _():
            block, part = at_chip * 2 + core, 2 * phase + half
            to_mate(block, part).wait_recv()

            @pl.when(goes_right(phase))
            def _():
                to_right(block, part).start()

            @pl.when(goes_mate(phase))
            def _():
                to_mate(block, part).start()

        there, at_chip, phase = from_right(turn)

        @pl.when(there)
        def _():
            block, part = at_chip * 2 + core, 2 * phase + half
            to_mate(block, part).wait_recv()

            @pl.when(goes_left(phase))
            def _():
                to_left(block, part).start()

            @pl.when(goes_mate(phase))
            def _():
                to_mate(block, part).start()

    turns = max(2 * high, chips + HELPED)
    answered = chips - HELPED

    def one_turn(turn, carry):
        pass_on(turn, 0)

        @pl.when(helper & (turn == answered + 1))
        def _():
            o_copy.start()

        there, at_chip, phase = from_left(turn - 1)

        @pl.when(there & (turn > 1))
        def _():
            take(at_chip, phase, 1)

        pass_on(turn, 1)

        @pl.when((turn == behind) & (chip < high))
        def _():
            own_sends(1, "right")

        @pl.when((turn == ahead) & (chip > low))
        def _():
            own_sends(1, "left")

        there, at_chip, phase = from_right(turn - 1)

        @pl.when(there & (turn > 1))
        def _():
            take(at_chip, phase, 1)

        @pl.when(helper & (turn == answered))
        def _():
            for n in range(2):
                put(o_out, n, 4 + n)
        return carry

    def put(target, place, tile):
        result = jnp.transpose(acc[tile] / totals[tile]).astype(jnp.bfloat16)
        for at in range(heads_per_tile):
            head = place * heads_per_tile + at
            target[:, head * HEAD_DIM:(head + 1) * HEAD_DIM] = result[at * new_rows:(at + 1) * new_rows]

    lax.fori_loop(1, turns + 2, one_turn, 0)

    for n in range(2):
        put(out_ref, n, n)

    @pl.when(inner)
    def _():
        for n in range(2, 4):
            put(out_ref, n, n)

    @pl.when(helped)
    def _():
        o_copy.wait_recv()
        out_ref[:, half_width:] = o_in[...]
        q_copy.wait_send()

    @pl.when(helper)
    def _():
        o_copy.wait_send()

    def finish(n, carry):
        at_chip, part = n // 4, n % 4
        phase = part // 2
        block = at_chip * 2 + core

        @pl.when(goes_left(phase) & (at_chip >= chip))
        def _():
            to_left(block, part).wait_send()

        @pl.when(goes_right(phase) & (at_chip <= chip))
        def _():
            to_right(block, part).wait_send()

        @pl.when(goes_mate(phase))
        def _():
            to_mate(block, part).wait_send()
        return carry

    lax.fori_loop(0, 4 * chips, finish, 0)


def local(queries, cache_keys, cache_values, new_keys, new_values, prefix_len):
    count = lax.axis_size("ctx")
    chips = count // 2
    rows, width = queries.shape
    key_rows = cache_keys.shape[0] + new_keys.shape[0]
    tiles = 6
    dma = pltpu.SemaphoreType.DMA
    anywhere = pl.BlockSpec(memory_space=pl.ANY)
    return pl.pallas_call(
        functools.partial(kernel, chips),
        out_shape=jax.ShapeDtypeStruct((rows, width), jnp.bfloat16),
        in_specs=[pl.BlockSpec(memory_space=pltpu.SMEM), pl.BlockSpec(memory_space=pltpu.VMEM)] + [anywhere] * 4,
        out_specs=pl.BlockSpec(memory_space=pltpu.VMEM),
        scratch_shapes=[
            pltpu.VMEM((count, 4, key_rows, HEAD_DIM), jnp.bfloat16),
            pltpu.VMEM((tiles, TILE, HEAD_DIM), jnp.bfloat16),
            pltpu.VMEM((tiles, 1, TILE), jnp.float32),
            pltpu.VMEM((tiles, 1, TILE), jnp.float32),
            pltpu.VMEM((tiles, HEAD_DIM, TILE), jnp.float32),
            pltpu.VMEM((rows, width // 2), jnp.bfloat16),
            pltpu.VMEM((rows, width // 2), jnp.bfloat16),
            pltpu.VMEM((rows, width // 2), jnp.bfloat16),
            dma((8,)), dma((chips, 4)), dma((chips, 4)), dma((chips, 4)), dma((count, 4)),
            dma((2,)), dma((2,)),
        ],
        compiler_params=pltpu.CompilerParams(collective_id=0, has_side_effects=True),
    )(prefix_len, queries, cache_keys, cache_values, new_keys, new_values)


def solution(mesh):
    spec = P(("dp", "ctx"), "tp")
    return jax.shard_map(
        local, mesh=mesh, in_specs=(spec,) * 5 + (P("dp"),), out_specs=spec, check_vma=False)
```

```python
import functools

import jax
import jax.numpy as jnp
from jax import lax
from jax.experimental import pallas as pl
from jax.experimental.pallas import tpu as pltpu
from jax.sharding import PartitionSpec as P

HEAD_DIM = 128
LOG2_E = 1.4426950408889634
MASKED = -1e30
TILE = 256


HELPED = 2
PIECES = 2


def kernel(chips, length_ref, q_ref, ck_ref, cv_ref, nk_ref, nv_ref, out_ref,
           held, qs, tops, totals, acc, q_in, o_in, o_out,
           local_sem, left_sem, right_sem, mate_sem, recv_sem, q_sems, o_sems):
    me = lax.axis_index("ctx")
    chip = me // 2
    core = me % 2
    last = chips - 1
    low, high = HELPED, last - HELPED
    inner = (chip >= low) & (chip <= high)
    helper = inner & ((chip < low + HELPED) | (chip > high - HELPED))
    helped_left, helped_right = chip < low, chip > high
    helped = helped_left | helped_right
    behind, ahead = chip, last - chip
    cache_rows = ck_ref.shape[0]
    new_rows = nk_ref.shape[0]
    key_rows = cache_rows + new_rows
    heads = q_ref.shape[1] // HEAD_DIM
    heads_per_tile = TILE // new_rows
    half_width = q_ref.shape[1] // 2
    length = length_ref[0]
    scale = (HEAD_DIM ** -0.5) * LOG2_E
    mate = chip * 2 + 1 - core
    lower = chip < chips // 2
    partner = me + jnp.where(lower == helped, 2 * HELPED, -2 * HELPED)

    loads = []
    for part in range(4):
        cached, fresh = ((ck_ref, nk_ref), (cv_ref, nv_ref))[part % 2]
        cols = pl.ds((1 - part // 2) * HEAD_DIM, HEAD_DIM)
        pair = (
            pltpu.make_async_copy(
                cached.at[:, cols], held.at[me, part, pl.ds(0, cache_rows)], local_sem.at[2 * part]),
            pltpu.make_async_copy(
                fresh.at[:, cols], held.at[me, part, pl.ds(cache_rows, new_rows)], local_sem.at[2 * part + 1]),
        )
        for load in pair:
            load.start()
        loads.append(pair)

    barrier = pltpu.get_barrier_semaphore()

    def greet(device):
        pl.semaphore_signal(barrier, inc=1, device_id={"ctx": device})

    greet(mate)

    @pl.when(chip > 0)
    def _():
        greet(me - 2)

    @pl.when(chip < last)
    def _():
        greet(me + 2)

    far = (helped | helper) & (HELPED > 1)

    @pl.when(far)
    def _():
        greet(partner)

    def as_int(flag):
        return flag.astype(jnp.int32)

    pl.semaphore_wait(
        barrier,
        1 + as_int(chip > 0) + as_int(chip < last) + as_int(far))

    q_copy = pltpu.make_async_remote_copy(
        src_ref=q_ref.at[:, pl.ds(half_width, half_width)], dst_ref=q_in,
        send_sem=q_sems.at[0], recv_sem=q_sems.at[1], device_id={"ctx": partner})
    o_copy = pltpu.make_async_remote_copy(
        src_ref=o_out, dst_ref=o_in,
        send_sem=o_sems.at[0], recv_sem=o_sems.at[1], device_id={"ctx": partner})

    @pl.when(helped)
    def _():
        q_copy.start()

    piece_rows = key_rows // PIECES

    def copy_of(block, part, sems, target, piece):
        rows = pl.ds(0, key_rows) if piece is None else pl.ds(piece * piece_rows, piece_rows)
        held_rows = held.at[block, part, rows]
        return pltpu.make_async_remote_copy(
            src_ref=held_rows, dst_ref=held_rows, send_sem=sems.at[block // 2, part],
            recv_sem=recv_sem.at[block, part * PIECES + (piece or 0)], device_id={"ctx": target})

    def to_left(block, part, piece=None):
        return copy_of(block, part, left_sem, me - 2, piece)

    def to_right(block, part, piece=None):
        return copy_of(block, part, right_sem, me + 2, piece)

    def to_mate(block, part, piece=None):
        return copy_of(block, part, mate_sem, mate, piece)

    def start_all(copy, part):
        for piece in range(PIECES):
            copy(me, part, piece).start()

    def goes_left(phase):
        return jnp.where(phase == 0, chip > low, chip > 0)

    def goes_right(phase):
        return jnp.where(phase == 0, chip < high, chip < last)

    def goes_mate(phase):
        return inner | (phase == 1)

    def compute(block, phase):
        def one_pair(pair, carry):
            keys = held[block, 2 * phase]
            values = held[block, 2 * phase + 1]
            asker = jnp.where(pair < 2, me, partner)
            both = [2 * pair, 2 * pair + 1]
            asked = [qs[n] for n in both]
            old_tops = [tops[n] for n in both]
            old_totals = [totals[n] for n in both]
            old_acc = [acc[n] for n in both]
            limit = length - block * cache_rows
            ahead_by = (block - asker) * new_rows
            row = lax.broadcasted_iota(jnp.int32, (cache_rows, TILE), 0)
            new_row = lax.broadcasted_iota(jnp.int32, (new_rows, TILE), 0)
            token = lax.broadcasted_iota(jnp.int32, (new_rows, TILE), 1) % new_rows
            stored = row < limit
            seen = new_row - token <= -ahead_by
            scores = [
                lax.dot_general(keys, q, (((1,), (1,)), ((), ())), preferred_element_type=jnp.float32) * scale
                for q in asked]
            results = []
            for n in range(2):
                cached = jnp.where(stored, scores[n][:cache_rows], MASKED)
                fresh = jnp.where(seen, scores[n][cache_rows:], MASKED)
                top = jnp.maximum(jnp.max(cached, 0, keepdims=True), jnp.max(fresh, 0, keepdims=True))
                top = jnp.maximum(old_tops[n], top)
                weights = jnp.exp2(jnp.concatenate([cached, fresh], 0) - top)
                rescale = jnp.exp2(old_tops[n] - top)
                total = old_totals[n] * rescale + jnp.sum(weights, 0, keepdims=True)
                part = lax.dot_general(
                    values, weights.astype(jnp.bfloat16), (((0,), (0,)), ((), ())),
                    preferred_element_type=jnp.float32)
                results.append((top, total, old_acc[n] * rescale + part))
            for n, (top, total, summed) in zip(both, results):
                tops[n] = top
                totals[n] = total
                acc[n] = summed
            return carry

        first = jnp.where(phase == 0, 1, 0)
        end = jnp.where(phase == 0, jnp.where(helper, 3, jnp.where(inner, 2, 1)), 1)
        lax.fori_loop(first, end, one_pair, 0)

    def own_sends(phase, direction):
        for part in (2 * phase, 2 * phase + 1):
            if direction == "left":
                start_all(to_left, part)
            else:
                start_all(to_right, part)

    for part in range(4):
        for load in loads[part]:
            load.wait()
        phase = part // 2
        if phase == 0:
            @pl.when(chip > low)
            def _():
                start_all(to_left, part)

            @pl.when(chip < high)
            def _():
                start_all(to_right, part)

            @pl.when(inner)
            def _():
                start_all(to_mate, part)
        else:
            @pl.when(((chip <= low) & (chip > 0)) | (chip == last))
            def _():
                start_all(to_left, part)

            @pl.when(((chip >= high) & (chip < last)) | (chip == 0))
            def _():
                start_all(to_right, part)

            start_all(to_mate, part)

    for head in range(heads):
        tile, at = divmod(head, heads_per_tile)
        qs[tile, at * new_rows:(at + 1) * new_rows, :] = q_ref[:, head * HEAD_DIM:(head + 1) * HEAD_DIM]
    tops[...] = jnp.full_like(tops, MASKED)
    totals[...] = jnp.zeros_like(totals)
    acc[...] = jnp.zeros_like(acc)

    @pl.when(helper)
    def _():
        q_copy.wait_recv()
        for head in range(heads // 2):
            tile, at = divmod(head, heads_per_tile)
            qs[4 + tile, at * new_rows:(at + 1) * new_rows, :] = q_in[:, head * HEAD_DIM:(head + 1) * HEAD_DIM]

    def take(at_chip, first_phase, phases):
        def one(n, carry):
            block = at_chip * 2 + jnp.where(n % 2 == 0, core, 1 - core)
            phase = first_phase + n // 2

            @pl.when(goes_mate(phase))
            def _():
                @pl.when(n % 2 == 1)
                def _():
                    for part in range(2):
                        for piece in range(PIECES):
                            to_mate(block, 2 * phase + part, piece).wait_recv()

                compute(block, phase)
            return carry
        lax.fori_loop(0, 2 * phases, one, 0)

    take(chip, 0, 1)

    def from_left(turn):
        late = turn - 2 * ahead
        phase = jnp.where(helped_right, 1, jnp.where(turn <= behind, 0, 1))
        step = jnp.where(helped_right, late, jnp.where(turn <= behind, turn, turn - behind))
        return (step >= 1) & (step <= behind), chip - step, phase

    def from_right(turn):
        late = turn - 2 * behind
        phase = jnp.where(helped_left, 1, jnp.where(turn <= ahead, 0, 1))
        step = jnp.where(helped_left, late, jnp.where(turn <= ahead, turn, turn - ahead))
        return (step >= 1) & (step <= ahead), chip + step, phase

    def pass_on(turn, half):
        for piece in range(PIECES):
            for coming, onward, goes in (
                (from_left, to_right, goes_right), (from_right, to_left, goes_left)):
                there, at_chip, phase = coming(turn)
                block, part = at_chip * 2 + core, 2 * phase + half

                @pl.when(there)
                def _():
                    to_mate(block, part, piece).wait_recv()

                    @pl.when(goes(phase))
                    def _():
                        onward(block, part, piece).start()

                    @pl.when(goes_mate(phase))
                    def _():
                        to_mate(block, part, piece).start()

    turns = max(2 * high, chips + HELPED)
    answered = chips - HELPED

    def one_turn(turn, carry):
        pass_on(turn, 0)

        @pl.when(helper & (turn == answered + 1))
        def _():
            o_copy.start()

        there, at_chip, phase = from_left(turn - 1)

        @pl.when(there | (turn == 1))
        def _():
            take(jnp.where(turn == 1, chip, at_chip), jnp.where(turn == 1, 1, phase), 1)

        pass_on(turn, 1)

        @pl.when((turn == behind) & (chip < high))
        def _():
            own_sends(1, "right")

        @pl.when((turn == ahead) & (chip > low))
        def _():
            own_sends(1, "left")

        there, at_chip, phase = from_right(turn - 1)

        @pl.when(there & (turn > 1))
        def _():
            take(at_chip, phase, 1)

        @pl.when(helper & (turn == answered))
        def _():
            for n in range(2):
                put(o_out, n, 4 + n)
        return carry

    def put(target, place, tile):
        result = jnp.transpose(acc[tile] / totals[tile]).astype(jnp.bfloat16)
        for at in range(heads_per_tile):
            head = place * heads_per_tile + at
            target[:, head * HEAD_DIM:(head + 1) * HEAD_DIM] = result[at * new_rows:(at + 1) * new_rows]

    lax.fori_loop(1, turns + 2, one_turn, 0)

    for n in range(2):
        put(out_ref, n, n)

    @pl.when(inner)
    def _():
        for n in range(2, 4):
            put(out_ref, n, n)

    @pl.when(helped)
    def _():
        o_copy.wait_recv()
        out_ref[:, half_width:] = o_in[...]
        q_copy.wait_send()

    @pl.when(helper)
    def _():
        o_copy.wait_send()

    def finish(n, carry):
        at_chip, part = n // 4, n % 4
        phase = part // 2
        block = at_chip * 2 + core

        @pl.when(goes_left(phase) & (at_chip >= chip))
        def _():
            to_left(block, part).wait_send()

        @pl.when(goes_right(phase) & (at_chip <= chip))
        def _():
            to_right(block, part).wait_send()

        @pl.when(goes_mate(phase))
        def _():
            to_mate(block, part).wait_send()
        return carry

    lax.fori_loop(0, 4 * chips, finish, 0)


def local(queries, cache_keys, cache_values, new_keys, new_values, prefix_len):
    count = lax.axis_size("ctx")
    chips = count // 2
    rows, width = queries.shape
    key_rows = cache_keys.shape[0] + new_keys.shape[0]
    tiles = 6
    dma = pltpu.SemaphoreType.DMA
    anywhere = pl.BlockSpec(memory_space=pl.ANY)
    return pl.pallas_call(
        functools.partial(kernel, chips),
        out_shape=jax.ShapeDtypeStruct((rows, width), jnp.bfloat16),
        in_specs=[pl.BlockSpec(memory_space=pltpu.SMEM), pl.BlockSpec(memory_space=pltpu.VMEM)] + [anywhere] * 4,
        out_specs=pl.BlockSpec(memory_space=pltpu.VMEM),
        scratch_shapes=[
            pltpu.VMEM((count, 4, key_rows, HEAD_DIM), jnp.bfloat16),
            pltpu.VMEM((tiles, TILE, HEAD_DIM), jnp.bfloat16),
            pltpu.VMEM((tiles, 1, TILE), jnp.float32),
            pltpu.VMEM((tiles, 1, TILE), jnp.float32),
            pltpu.VMEM((tiles, HEAD_DIM, TILE), jnp.float32),
            pltpu.VMEM((rows, width // 2), jnp.bfloat16),
            pltpu.VMEM((rows, width // 2), jnp.bfloat16),
            pltpu.VMEM((rows, width // 2), jnp.bfloat16),
            dma((8,)), dma((chips, 4)), dma((chips, 4)), dma((chips, 4)), dma((count, 4 * PIECES)),
            dma((2,)), dma((2,)),
        ],
        compiler_params=pltpu.CompilerParams(collective_id=0, has_side_effects=True),
    )(prefix_len, queries, cache_keys, cache_values, new_keys, new_values)


def solution(mesh):
    spec = P(("dp", "ctx"), "tp")
    return jax.shard_map(
        local, mesh=mesh, in_specs=(spec,) * 5 + (P("dp"),), out_specs=spec, check_vma=False)
```

```python
import functools

import jax
import jax.numpy as jnp
from jax import lax
from jax.experimental import pallas as pl
from jax.experimental.pallas import tpu as pltpu
from jax.sharding import PartitionSpec as P

HEAD_DIM = 128
LOG2_E = 1.4426950408889634
MASKED = -1e30
TILE = 256


HELPED = 1
PIECES = 2


def kernel(chips, length_ref, q_ref, ck_ref, cv_ref, nk_ref, nv_ref, out_ref,
           held, qs, tops, totals, acc, q_in, o_in, o_out,
           local_sem, left_sem, right_sem, mate_sem, recv_sem, q_sems, o_sems):
    me = lax.axis_index("ctx")
    chip = me // 2
    core = me % 2
    last = chips - 1
    low, high = HELPED, last - HELPED
    inner = (chip >= low) & (chip <= high)
    helper = inner & ((chip < low + HELPED) | (chip > high - HELPED))
    helped_left, helped_right = chip < low, chip > high
    helped = helped_left | helped_right
    behind, ahead = chip, last - chip
    cache_rows = ck_ref.shape[0]
    new_rows = nk_ref.shape[0]
    key_rows = cache_rows + new_rows
    heads = q_ref.shape[1] // HEAD_DIM
    heads_per_tile = TILE // new_rows
    half_width = q_ref.shape[1] // 2
    length = length_ref[0]
    scale = (HEAD_DIM ** -0.5) * LOG2_E
    mate = chip * 2 + 1 - core
    lower = chip < chips // 2
    partner = me + jnp.where(lower == helped, 2 * HELPED, -2 * HELPED)

    loads = []
    for part in range(4):
        cached, fresh = ((ck_ref, nk_ref), (cv_ref, nv_ref))[part % 2]
        cols = pl.ds((1 - part // 2) * HEAD_DIM, HEAD_DIM)
        pair = (
            pltpu.make_async_copy(
                cached.at[:, cols], held.at[me, part, pl.ds(0, cache_rows)], local_sem.at[2 * part]),
            pltpu.make_async_copy(
                fresh.at[:, cols], held.at[me, part, pl.ds(cache_rows, new_rows)], local_sem.at[2 * part + 1]),
        )
        for load in pair:
            load.start()
        loads.append(pair)

    barrier = pltpu.get_barrier_semaphore()

    def greet(device):
        pl.semaphore_signal(barrier, inc=1, device_id={"ctx": device})

    greet(mate)

    @pl.when(chip > 0)
    def _():
        greet(me - 2)

    @pl.when(chip < last)
    def _():
        greet(me + 2)

    far = (helped | helper) & (HELPED > 1)

    @pl.when(far)
    def _():
        greet(partner)

    def as_int(flag):
        return flag.astype(jnp.int32)

    pl.semaphore_wait(
        barrier,
        1 + as_int(chip > 0) + as_int(chip < last) + as_int(far))

    q_copy = pltpu.make_async_remote_copy(
        src_ref=q_ref.at[:, pl.ds(half_width, half_width)], dst_ref=q_in,
        send_sem=q_sems.at[0], recv_sem=q_sems.at[1], device_id={"ctx": partner})
    o_copy = pltpu.make_async_remote_copy(
        src_ref=o_out, dst_ref=o_in,
        send_sem=o_sems.at[0], recv_sem=o_sems.at[1], device_id={"ctx": partner})

    @pl.when(helped)
    def _():
        q_copy.start()

    piece_rows = key_rows // PIECES

    def copy_of(block, part, sems, target, piece):
        rows = pl.ds(0, key_rows) if piece is None else pl.ds(piece * piece_rows, piece_rows)
        held_rows = held.at[block, part, rows]
        return pltpu.make_async_remote_copy(
            src_ref=held_rows, dst_ref=held_rows, send_sem=sems.at[block // 2, part],
            recv_sem=recv_sem.at[block, part * PIECES + (piece or 0)], device_id={"ctx": target})

    def to_left(block, part, piece=None):
        return copy_of(block, part, left_sem, me - 2, piece)

    def to_right(block, part, piece=None):
        return copy_of(block, part, right_sem, me + 2, piece)

    def to_mate(block, part, piece=None):
        return copy_of(block, part, mate_sem, mate, piece)

    def start_all(copy, part):
        for piece in range(PIECES):
            copy(me, part, piece).start()

    def goes_left(phase):
        return jnp.where(phase == 0, chip > low, chip > 0)

    def goes_right(phase):
        return jnp.where(phase == 0, chip < high, chip < last)

    def goes_mate(phase):
        return inner | (phase == 1)

    def compute(block, phase):
        def one_pair(pair, carry):
            keys = held[block, 2 * phase]
            values = held[block, 2 * phase + 1]
            asker = jnp.where(pair < 2, me, partner)
            both = [2 * pair, 2 * pair + 1]
            asked = [qs[n] for n in both]
            old_tops = [tops[n] for n in both]
            old_totals = [totals[n] for n in both]
            old_acc = [acc[n] for n in both]
            limit = length - block * cache_rows
            ahead_by = (block - asker) * new_rows
            row = lax.broadcasted_iota(jnp.int32, (cache_rows, TILE), 0)
            new_row = lax.broadcasted_iota(jnp.int32, (new_rows, TILE), 0)
            token = lax.broadcasted_iota(jnp.int32, (new_rows, TILE), 1) % new_rows
            stored = row < limit
            seen = new_row - token <= -ahead_by
            scores = [
                lax.dot_general(keys, q, (((1,), (1,)), ((), ())), preferred_element_type=jnp.float32) * scale
                for q in asked]
            results = []
            for n in range(2):
                cached = jnp.where(stored, scores[n][:cache_rows], MASKED)
                fresh = jnp.where(seen, scores[n][cache_rows:], MASKED)
                top = jnp.maximum(jnp.max(cached, 0, keepdims=True), jnp.max(fresh, 0, keepdims=True))
                top = jnp.maximum(old_tops[n], top)
                weights = jnp.exp2(jnp.concatenate([cached, fresh], 0) - top)
                rescale = jnp.exp2(old_tops[n] - top)
                total = old_totals[n] * rescale + jnp.sum(weights, 0, keepdims=True)
                part = lax.dot_general(
                    values, weights.astype(jnp.bfloat16), (((0,), (0,)), ((), ())),
                    preferred_element_type=jnp.float32)
                results.append((top, total, old_acc[n] * rescale + part))
            for n, (top, total, summed) in zip(both, results):
                tops[n] = top
                totals[n] = total
                acc[n] = summed
            return carry

        first = jnp.where(phase == 0, 1, 0)
        end = jnp.where(phase == 0, jnp.where(helper, 3, jnp.where(inner, 2, 1)), 1)
        lax.fori_loop(first, end, one_pair, 0)

    def own_sends(phase, direction):
        for part in (2 * phase, 2 * phase + 1):
            if direction == "left":
                start_all(to_left, part)
            else:
                start_all(to_right, part)

    for part in range(4):
        for load in loads[part]:
            load.wait()
        phase = part // 2
        if phase == 0:
            @pl.when(chip > low)
            def _():
                start_all(to_left, part)

            @pl.when(chip < high)
            def _():
                start_all(to_right, part)

            @pl.when(inner)
            def _():
                start_all(to_mate, part)
        else:
            @pl.when(((chip <= low) & (chip > 0)) | (chip == last))
            def _():
                start_all(to_left, part)

            @pl.when(((chip >= high) & (chip < last)) | (chip == 0))
            def _():
                start_all(to_right, part)

            start_all(to_mate, part)

    for head in range(heads):
        tile, at = divmod(head, heads_per_tile)
        qs[tile, at * new_rows:(at + 1) * new_rows, :] = q_ref[:, head * HEAD_DIM:(head + 1) * HEAD_DIM]
    tops[...] = jnp.full_like(tops, MASKED)
    totals[...] = jnp.zeros_like(totals)
    acc[...] = jnp.zeros_like(acc)

    @pl.when(helper)
    def _():
        q_copy.wait_recv()
        for head in range(heads // 2):
            tile, at = divmod(head, heads_per_tile)
            qs[4 + tile, at * new_rows:(at + 1) * new_rows, :] = q_in[:, head * HEAD_DIM:(head + 1) * HEAD_DIM]

    def take(at_chip, first_phase, phases):
        def one(n, carry):
            block = at_chip * 2 + jnp.where(n % 2 == 0, core, 1 - core)
            phase = first_phase + n // 2

            @pl.when(goes_mate(phase))
            def _():
                @pl.when(n % 2 == 1)
                def _():
                    for part in range(2):
                        for piece in range(PIECES):
                            to_mate(block, 2 * phase + part, piece).wait_recv()

                compute(block, phase)
            return carry
        lax.fori_loop(0, 2 * phases, one, 0)

    take(chip, 0, 1)

    def from_left(turn):
        late = turn - 2 * ahead
        phase = jnp.where(helped_right, 1, jnp.where(turn <= behind, 0, 1))
        step = jnp.where(helped_right, late, jnp.where(turn <= behind, turn, turn - behind))
        return (step >= 1) & (step <= behind), chip - step, phase

    def from_right(turn):
        late = turn - 2 * behind
        phase = jnp.where(helped_left, 1, jnp.where(turn <= ahead, 0, 1))
        step = jnp.where(helped_left, late, jnp.where(turn <= ahead, turn, turn - ahead))
        return (step >= 1) & (step <= ahead), chip + step, phase

    def pass_on(turn, half):
        for piece in range(PIECES):
            for coming, onward, goes in (
                (from_left, to_right, goes_right), (from_right, to_left, goes_left)):
                there, at_chip, phase = coming(turn)
                block, part = at_chip * 2 + core, 2 * phase + half

                @pl.when(there)
                def _():
                    to_mate(block, part, piece).wait_recv()

                    @pl.when(goes(phase))
                    def _():
                        onward(block, part, piece).start()

                    @pl.when(goes_mate(phase))
                    def _():
                        to_mate(block, part, piece).start()

    turns = max(2 * high, chips + HELPED)
    answered = chips - HELPED

    def one_turn(turn, carry):
        pass_on(turn, 0)

        @pl.when(helper & (turn == answered + 1))
        def _():
            o_copy.start()

        there, at_chip, phase = from_left(turn - 1)

        @pl.when(there | (turn == 1))
        def _():
            take(jnp.where(turn == 1, chip, at_chip), jnp.where(turn == 1, 1, phase), 1)

        pass_on(turn, 1)

        @pl.when((turn == behind) & (chip < high))
        def _():
            own_sends(1, "right")

        @pl.when((turn == ahead) & (chip > low))
        def _():
            own_sends(1, "left")

        there, at_chip, phase = from_right(turn - 1)

        @pl.when(there & (turn > 1))
        def _():
            take(at_chip, phase, 1)

        @pl.when(helper & (turn == answered))
        def _():
            for n in range(2):
                put(o_out, n, 4 + n)
        return carry

    def put(target, place, tile):
        result = jnp.transpose(acc[tile] / totals[tile]).astype(jnp.bfloat16)
        for at in range(heads_per_tile):
            head = place * heads_per_tile + at
            target[:, head * HEAD_DIM:(head + 1) * HEAD_DIM] = result[at * new_rows:(at + 1) * new_rows]

    lax.fori_loop(1, turns + 2, one_turn, 0)

    for n in range(2):
        put(out_ref, n, n)

    @pl.when(inner)
    def _():
        for n in range(2, 4):
            put(out_ref, n, n)

    @pl.when(helped)
    def _():
        o_copy.wait_recv()
        out_ref[:, half_width:] = o_in[...]
        q_copy.wait_send()

    @pl.when(helper)
    def _():
        o_copy.wait_send()

    def finish(n, carry):
        at_chip, part = n // 4, n % 4
        phase = part // 2
        block = at_chip * 2 + core

        @pl.when(goes_left(phase) & (at_chip >= chip))
        def _():
            to_left(block, part).wait_send()

        @pl.when(goes_right(phase) & (at_chip <= chip))
        def _():
            to_right(block, part).wait_send()

        @pl.when(goes_mate(phase))
        def _():
            to_mate(block, part).wait_send()
        return carry

    lax.fori_loop(0, 4 * chips, finish, 0)


def local(queries, cache_keys, cache_values, new_keys, new_values, prefix_len):
    count = lax.axis_size("ctx")
    chips = count // 2
    rows, width = queries.shape
    key_rows = cache_keys.shape[0] + new_keys.shape[0]
    tiles = 6
    dma = pltpu.SemaphoreType.DMA
    anywhere = pl.BlockSpec(memory_space=pl.ANY)
    return pl.pallas_call(
        functools.partial(kernel, chips),
        out_shape=jax.ShapeDtypeStruct((rows, width), jnp.bfloat16),
        in_specs=[pl.BlockSpec(memory_space=pltpu.SMEM), pl.BlockSpec(memory_space=pltpu.VMEM)] + [anywhere] * 4,
        out_specs=pl.BlockSpec(memory_space=pltpu.VMEM),
        scratch_shapes=[
            pltpu.VMEM((count, 4, key_rows, HEAD_DIM), jnp.bfloat16),
            pltpu.VMEM((tiles, TILE, HEAD_DIM), jnp.bfloat16),
            pltpu.VMEM((tiles, 1, TILE), jnp.float32),
            pltpu.VMEM((tiles, 1, TILE), jnp.float32),
            pltpu.VMEM((tiles, HEAD_DIM, TILE), jnp.float32),
            pltpu.VMEM((rows, width // 2), jnp.bfloat16),
            pltpu.VMEM((rows, width // 2), jnp.bfloat16),
            pltpu.VMEM((rows, width // 2), jnp.bfloat16),
            dma((8,)), dma((chips, 4)), dma((chips, 4)), dma((chips, 4)), dma((count, 4 * PIECES)),
            dma((2,)), dma((2,)),
        ],
        compiler_params=pltpu.CompilerParams(collective_id=0, has_side_effects=True),
    )(prefix_len, queries, cache_keys, cache_values, new_keys, new_values)


def solution(mesh):
    spec = P(("dp", "ctx"), "tp")
    return jax.shard_map(
        local, mesh=mesh, in_specs=(spec,) * 5 + (P("dp"),), out_specs=spec, check_vma=False)
```

```python
import functools

import jax
import jax.numpy as jnp
from jax import lax
from jax.experimental import pallas as pl
from jax.experimental.pallas import tpu as pltpu
from jax.sharding import PartitionSpec as P

HEAD_DIM = 128
LOG2_E = 1.4426950408889634
MASKED = -1e30
TILE = 256


HELPED = 1
PIECES = 4


def kernel(chips, length_ref, q_ref, ck_ref, cv_ref, nk_ref, nv_ref, out_ref,
           held, qs, tops, totals, acc, q_in, o_in, o_out,
           local_sem, left_sem, right_sem, mate_sem, recv_sem, q_sems, o_sems):
    me = lax.axis_index("ctx")
    chip = me // 2
    core = me % 2
    last = chips - 1
    low, high = HELPED, last - HELPED
    inner = (chip >= low) & (chip <= high)
    helper = inner & ((chip < low + HELPED) | (chip > high - HELPED))
    helped_left, helped_right = chip < low, chip > high
    helped = helped_left | helped_right
    behind, ahead = chip, last - chip
    cache_rows = ck_ref.shape[0]
    new_rows = nk_ref.shape[0]
    key_rows = cache_rows + new_rows
    heads = q_ref.shape[1] // HEAD_DIM
    heads_per_tile = TILE // new_rows
    half_width = q_ref.shape[1] // 2
    length = length_ref[0]
    scale = (HEAD_DIM ** -0.5) * LOG2_E
    mate = chip * 2 + 1 - core
    lower = chip < chips // 2
    partner = me + jnp.where(lower == helped, 2 * HELPED, -2 * HELPED)

    loads = []
    for part in range(4):
        cached, fresh = ((ck_ref, nk_ref), (cv_ref, nv_ref))[part % 2]
        cols = pl.ds((1 - part // 2) * HEAD_DIM, HEAD_DIM)
        pair = (
            pltpu.make_async_copy(
                cached.at[:, cols], held.at[me, part, pl.ds(0, cache_rows)], local_sem.at[2 * part]),
            pltpu.make_async_copy(
                fresh.at[:, cols], held.at[me, part, pl.ds(cache_rows, new_rows)], local_sem.at[2 * part + 1]),
        )
        for load in pair:
            load.start()
        loads.append(pair)

    barrier = pltpu.get_barrier_semaphore()

    def greet(device):
        pl.semaphore_signal(barrier, inc=1, device_id={"ctx": device})

    greet(mate)

    @pl.when(chip > 0)
    def _():
        greet(me - 2)

    @pl.when(chip < last)
    def _():
        greet(me + 2)

    far = (helped | helper) & (HELPED > 1)

    @pl.when(far)
    def _():
        greet(partner)

    def as_int(flag):
        return flag.astype(jnp.int32)

    pl.semaphore_wait(
        barrier,
        1 + as_int(chip > 0) + as_int(chip < last) + as_int(far))

    q_copy = pltpu.make_async_remote_copy(
        src_ref=q_ref.at[:, pl.ds(half_width, half_width)], dst_ref=q_in,
        send_sem=q_sems.at[0], recv_sem=q_sems.at[1], device_id={"ctx": partner})
    o_copy = pltpu.make_async_remote_copy(
        src_ref=o_out, dst_ref=o_in,
        send_sem=o_sems.at[0], recv_sem=o_sems.at[1], device_id={"ctx": partner})

    @pl.when(helped)
    def _():
        q_copy.start()

    piece_rows = key_rows // PIECES

    def copy_of(block, part, sems, target, piece):
        rows = pl.ds(0, key_rows) if piece is None else pl.ds(piece * piece_rows, piece_rows)
        held_rows = held.at[block, part, rows]
        return pltpu.make_async_remote_copy(
            src_ref=held_rows, dst_ref=held_rows, send_sem=sems.at[block // 2, part],
            recv_sem=recv_sem.at[block, part * PIECES + (piece or 0)], device_id={"ctx": target})

    def to_left(block, part, piece=None):
        return copy_of(block, part, left_sem, me - 2, piece)

    def to_right(block, part, piece=None):
        return copy_of(block, part, right_sem, me + 2, piece)

    def to_mate(block, part, piece=None):
        return copy_of(block, part, mate_sem, mate, piece)

    def start_all(copy, part):
        for piece in range(PIECES):
            copy(me, part, piece).start()

    def goes_left(phase):
        return jnp.where(phase == 0, chip > low, chip > 0)

    def goes_right(phase):
        return jnp.where(phase == 0, chip < high, chip < last)

    def goes_mate(phase):
        return inner | (phase == 1)

    def compute(block, phase):
        def one_pair(pair, carry):
            keys = held[block, 2 * phase]
            values = held[block, 2 * phase + 1]
            asker = jnp.where(pair < 2, me, partner)
            both = [2 * pair, 2 * pair + 1]
            asked = [qs[n] for n in both]
            old_tops = [tops[n] for n in both]
            old_totals = [totals[n] for n in both]
            old_acc = [acc[n] for n in both]
            limit = length - block * cache_rows
            ahead_by = (block - asker) * new_rows
            row = lax.broadcasted_iota(jnp.int32, (cache_rows, TILE), 0)
            new_row = lax.broadcasted_iota(jnp.int32, (new_rows, TILE), 0)
            token = lax.broadcasted_iota(jnp.int32, (new_rows, TILE), 1) % new_rows
            stored = row < limit
            seen = new_row - token <= -ahead_by
            scores = [
                lax.dot_general(keys, q, (((1,), (1,)), ((), ())), preferred_element_type=jnp.float32) * scale
                for q in asked]
            results = []
            for n in range(2):
                cached = jnp.where(stored, scores[n][:cache_rows], MASKED)
                fresh = jnp.where(seen, scores[n][cache_rows:], MASKED)
                top = jnp.maximum(jnp.max(cached, 0, keepdims=True), jnp.max(fresh, 0, keepdims=True))
                top = jnp.maximum(old_tops[n], top)
                weights = jnp.exp2(jnp.concatenate([cached, fresh], 0) - top)
                rescale = jnp.exp2(old_tops[n] - top)
                total = old_totals[n] * rescale + jnp.sum(weights, 0, keepdims=True)
                part = lax.dot_general(
                    values, weights.astype(jnp.bfloat16), (((0,), (0,)), ((), ())),
                    preferred_element_type=jnp.float32)
                results.append((top, total, old_acc[n] * rescale + part))
            for n, (top, total, summed) in zip(both, results):
                tops[n] = top
                totals[n] = total
                acc[n] = summed
            return carry

        first = jnp.where(phase == 0, 1, 0)
        end = jnp.where(phase == 0, jnp.where(helper, 3, jnp.where(inner, 2, 1)), 1)
        lax.fori_loop(first, end, one_pair, 0)

    def own_sends(phase, direction):
        for part in (2 * phase, 2 * phase + 1):
            if direction == "left":
                start_all(to_left, part)
            else:
                start_all(to_right, part)

    for part in range(4):
        for load in loads[part]:
            load.wait()
        phase = part // 2
        if phase == 0:
            @pl.when(chip > low)
            def _():
                start_all(to_left, part)

            @pl.when(chip < high)
            def _():
                start_all(to_right, part)

            @pl.when(inner)
            def _():
                start_all(to_mate, part)
        else:
            @pl.when(((chip <= low) & (chip > 0)) | (chip == last))
            def _():
                start_all(to_left, part)

            @pl.when(((chip >= high) & (chip < last)) | (chip == 0))
            def _():
                start_all(to_right, part)

            start_all(to_mate, part)

    for head in range(heads):
        tile, at = divmod(head, heads_per_tile)
        qs[tile, at * new_rows:(at + 1) * new_rows, :] = q_ref[:, head * HEAD_DIM:(head + 1) * HEAD_DIM]
    tops[...] = jnp.full_like(tops, MASKED)
    totals[...] = jnp.zeros_like(totals)
    acc[...] = jnp.zeros_like(acc)

    @pl.when(helper)
    def _():
        q_copy.wait_recv()
        for head in range(heads // 2):
            tile, at = divmod(head, heads_per_tile)
            qs[4 + tile, at * new_rows:(at + 1) * new_rows, :] = q_in[:, head * HEAD_DIM:(head + 1) * HEAD_DIM]

    def take(at_chip, first_phase, phases):
        def one(n, carry):
            block = at_chip * 2 + jnp.where(n % 2 == 0, core, 1 - core)
            phase = first_phase + n // 2

            @pl.when(goes_mate(phase))
            def _():
                @pl.when(n % 2 == 1)
                def _():
                    for part in range(2):
                        for piece in range(PIECES):
                            to_mate(block, 2 * phase + part, piece).wait_recv()

                compute(block, phase)
            return carry
        lax.fori_loop(0, 2 * phases, one, 0)

    take(chip, 0, 1)

    def from_left(turn):
        late = turn - 2 * ahead
        phase = jnp.where(helped_right, 1, jnp.where(turn <= behind, 0, 1))
        step = jnp.where(helped_right, late, jnp.where(turn <= behind, turn, turn - behind))
        return (step >= 1) & (step <= behind), chip - step, phase

    def from_right(turn):
        late = turn - 2 * behind
        phase = jnp.where(helped_left, 1, jnp.where(turn <= ahead, 0, 1))
        step = jnp.where(helped_left, late, jnp.where(turn <= ahead, turn, turn - ahead))
        return (step >= 1) & (step <= ahead), chip + step, phase

    def pass_on(turn, half):
        for piece in range(PIECES):
            for coming, onward, goes in (
                (from_left, to_right, goes_right), (from_right, to_left, goes_left)):
                there, at_chip, phase = coming(turn)
                block, part = at_chip * 2 + core, 2 * phase + half

                @pl.when(there)
                def _():
                    to_mate(block, part, piece).wait_recv()

                    @pl.when(goes(phase))
                    def _():
                        onward(block, part, piece).start()

                    @pl.when(goes_mate(phase))
                    def _():
                        to_mate(block, part, piece).start()

    turns = max(2 * high, chips + HELPED)
    answered = chips - HELPED

    def one_turn(turn, carry):
        pass_on(turn, 0)

        @pl.when(helper & (turn == answered + 1))
        def _():
            o_copy.start()

        there, at_chip, phase = from_left(turn - 1)

        @pl.when(there | (turn == 1))
        def _():
            take(jnp.where(turn == 1, chip, at_chip), jnp.where(turn == 1, 1, phase), 1)

        pass_on(turn, 1)

        @pl.when((turn == behind) & (chip < high))
        def _():
            own_sends(1, "right")

        @pl.when((turn == ahead) & (chip > low))
        def _():
            own_sends(1, "left")

        there, at_chip, phase = from_right(turn - 1)

        @pl.when(there & (turn > 1))
        def _():
            take(at_chip, phase, 1)

        @pl.when(helper & (turn == answered))
        def _():
            for n in range(2):
                put(o_out, n, 4 + n)

        @pl.when(inner & (turn == answered + 1))
        def _():
            for n in range(2, 4):
                put(out_ref, n, n)
        return carry

    def put(target, place, tile):
        result = jnp.transpose(acc[tile] / totals[tile]).astype(jnp.bfloat16)
        for at in range(heads_per_tile):
            head = place * heads_per_tile + at
            target[:, head * HEAD_DIM:(head + 1) * HEAD_DIM] = result[at * new_rows:(at + 1) * new_rows]

    lax.fori_loop(1, turns + 2, one_turn, 0)

    for n in range(2):
        put(out_ref, n, n)

    @pl.when(helped)
    def _():
        o_copy.wait_recv()
        out_ref[:, half_width:] = o_in[...]
        q_copy.wait_send()

    @pl.when(helper)
    def _():
        o_copy.wait_send()

    def finish(n, carry):
        at_chip, part = n // 4, n % 4
        phase = part // 2
        block = at_chip * 2 + core

        @pl.when(goes_left(phase) & (at_chip >= chip))
        def _():
            to_left(block, part).wait_send()

        @pl.when(goes_right(phase) & (at_chip <= chip))
        def _():
            to_right(block, part).wait_send()

        @pl.when(goes_mate(phase))
        def _():
            to_mate(block, part).wait_send()
        return carry

    lax.fori_loop(0, 4 * chips, finish, 0)


def local(queries, cache_keys, cache_values, new_keys, new_values, prefix_len):
    count = lax.axis_size("ctx")
    chips = count // 2
    rows, width = queries.shape
    key_rows = cache_keys.shape[0] + new_keys.shape[0]
    tiles = 6
    dma = pltpu.SemaphoreType.DMA
    anywhere = pl.BlockSpec(memory_space=pl.ANY)
    return pl.pallas_call(
        functools.partial(kernel, chips),
        out_shape=jax.ShapeDtypeStruct((rows, width), jnp.bfloat16),
        in_specs=[pl.BlockSpec(memory_space=pltpu.SMEM), pl.BlockSpec(memory_space=pltpu.VMEM)] + [anywhere] * 4,
        out_specs=pl.BlockSpec(memory_space=pltpu.VMEM),
        scratch_shapes=[
            pltpu.VMEM((count, 4, key_rows, HEAD_DIM), jnp.bfloat16),
            pltpu.VMEM((tiles, TILE, HEAD_DIM), jnp.bfloat16),
            pltpu.VMEM((tiles, 1, TILE), jnp.float32),
            pltpu.VMEM((tiles, 1, TILE), jnp.float32),
            pltpu.VMEM((tiles, HEAD_DIM, TILE), jnp.float32),
            pltpu.VMEM((rows, width // 2), jnp.bfloat16),
            pltpu.VMEM((rows, width // 2), jnp.bfloat16),
            pltpu.VMEM((rows, width // 2), jnp.bfloat16),
            dma((8,)), dma((chips, 4)), dma((chips, 4)), dma((chips, 4)), dma((count, 4 * PIECES)),
            dma((2,)), dma((2,)),
        ],
        compiler_params=pltpu.CompilerParams(collective_id=0, has_side_effects=True),
    )(prefix_len, queries, cache_keys, cache_values, new_keys, new_values)


def solution(mesh):
    spec = P(("dp", "ctx"), "tp")
    return jax.shard_map(
        local, mesh=mesh, in_specs=(spec,) * 5 + (P("dp"),), out_specs=spec, check_vma=False)
```

```python
import functools

import jax
import jax.numpy as jnp
from jax import lax
from jax.experimental import pallas as pl
from jax.experimental.pallas import tpu as pltpu
from jax.sharding import PartitionSpec as P

HEAD_DIM = 128
LOG2_E = 1.4426950408889634
MASKED = -1e30
TILE = 256


HELPED = 1
PIECES = 2


def kernel(chips, length_ref, q_ref, ck_ref, cv_ref, nk_ref, nv_ref, out_ref,
           held, qs, tops, totals, acc, q_in, o_in, o_out,
           local_sem, left_sem, right_sem, mate_sem, recv_sem, q_sems, o_sems):
    me = lax.axis_index("ctx")
    chip = me // 2
    core = me % 2
    last = chips - 1
    low, high = HELPED, last - HELPED
    inner = (chip >= low) & (chip <= high)
    helper = inner & ((chip < low + HELPED) | (chip > high - HELPED))
    helped_left, helped_right = chip < low, chip > high
    helped = helped_left | helped_right
    behind, ahead = chip, last - chip
    cache_rows = ck_ref.shape[0]
    new_rows = nk_ref.shape[0]
    key_rows = cache_rows + new_rows
    heads = q_ref.shape[1] // HEAD_DIM
    heads_per_tile = TILE // new_rows
    half_width = q_ref.shape[1] // 2
    length = length_ref[0]
    scale = (HEAD_DIM ** -0.5) * LOG2_E
    mate = chip * 2 + 1 - core
    lower = chip < chips // 2
    partner = me + jnp.where(lower == helped, 2 * HELPED, -2 * HELPED)

    loads = []
    for part in range(4):
        cached, fresh = ((ck_ref, nk_ref), (cv_ref, nv_ref))[part % 2]
        cols = pl.ds((1 - part // 2) * HEAD_DIM, HEAD_DIM)
        pair = (
            pltpu.make_async_copy(
                cached.at[:, cols], held.at[me, part, pl.ds(0, cache_rows)], local_sem.at[2 * part]),
            pltpu.make_async_copy(
                fresh.at[:, cols], held.at[me, part, pl.ds(cache_rows, new_rows)], local_sem.at[2 * part + 1]),
        )
        for load in pair:
            load.start()
        loads.append(pair)

    barrier = pltpu.get_barrier_semaphore()

    def greet(device):
        pl.semaphore_signal(barrier, inc=1, device_id={"ctx": device})

    greet(mate)

    @pl.when(chip > 0)
    def _():
        greet(me - 2)

    @pl.when(chip < last)
    def _():
        greet(me + 2)

    far = (helped | helper) & (HELPED > 1)

    @pl.when(far)
    def _():
        greet(partner)

    def as_int(flag):
        return flag.astype(jnp.int32)

    pl.semaphore_wait(
        barrier,
        1 + as_int(chip > 0) + as_int(chip < last) + as_int(far))

    q_copy = pltpu.make_async_remote_copy(
        src_ref=q_ref.at[:, pl.ds(half_width, half_width)], dst_ref=q_in,
        send_sem=q_sems.at[0], recv_sem=q_sems.at[1], device_id={"ctx": partner})
    o_copy = pltpu.make_async_remote_copy(
        src_ref=o_out, dst_ref=o_in,
        send_sem=o_sems.at[0], recv_sem=o_sems.at[1], device_id={"ctx": partner})

    @pl.when(helped)
    def _():
        q_copy.start()

    piece_rows = key_rows // PIECES

    def copy_of(block, part, sems, target, piece):
        rows = pl.ds(0, key_rows) if piece is None else pl.ds(piece * piece_rows, piece_rows)
        held_rows = held.at[block, part, rows]
        return pltpu.make_async_remote_copy(
            src_ref=held_rows, dst_ref=held_rows, send_sem=sems.at[block // 2, part],
            recv_sem=recv_sem.at[block, part * PIECES + (piece or 0)], device_id={"ctx": target})

    def to_left(block, part, piece=None):
        return copy_of(block, part, left_sem, me - 2, piece)

    def to_right(block, part, piece=None):
        return copy_of(block, part, right_sem, me + 2, piece)

    def to_mate(block, part, piece=None):
        return copy_of(block, part, mate_sem, mate, piece)

    def start_all(copy, part):
        for piece in range(PIECES):
            copy(me, part, piece).start()

    def goes_left(phase):
        return jnp.where(phase == 0, chip > low, chip > 0)

    def goes_right(phase):
        return jnp.where(phase == 0, chip < high, chip < last)

    def goes_mate(phase):
        return inner | (phase == 1)

    def compute(block, phase):
        def one_pair(pair, carry):
            keys = held[block, 2 * phase]
            values = held[block, 2 * phase + 1]
            asker = jnp.where(pair < 2, me, partner)
            both = [2 * pair, 2 * pair + 1]
            asked = [qs[n] for n in both]
            old_tops = [tops[n] for n in both]
            old_totals = [totals[n] for n in both]
            old_acc = [acc[n] for n in both]
            limit = length - block * cache_rows
            ahead_by = (block - asker) * new_rows
            row = lax.broadcasted_iota(jnp.int32, (cache_rows, TILE), 0)
            new_row = lax.broadcasted_iota(jnp.int32, (new_rows, TILE), 0)
            token = lax.broadcasted_iota(jnp.int32, (new_rows, TILE), 1) % new_rows
            stored = row < limit
            seen = new_row - token <= -ahead_by
            scores = [
                lax.dot_general(keys, q, (((1,), (1,)), ((), ())), preferred_element_type=jnp.float32) * scale
                for q in asked]
            results = []
            for n in range(2):
                cached = jnp.where(stored, scores[n][:cache_rows], MASKED)
                fresh = jnp.where(seen, scores[n][cache_rows:], MASKED)
                top = jnp.maximum(jnp.max(cached, 0, keepdims=True), jnp.max(fresh, 0, keepdims=True))
                top = jnp.maximum(old_tops[n], top)
                weights = jnp.exp2(jnp.concatenate([cached, fresh], 0) - top)
                rescale = jnp.exp2(old_tops[n] - top)
                total = old_totals[n] * rescale + jnp.sum(weights, 0, keepdims=True)
                part = lax.dot_general(
                    values, weights.astype(jnp.bfloat16), (((0,), (0,)), ((), ())),
                    preferred_element_type=jnp.float32)
                results.append((top, total, old_acc[n] * rescale + part))
            for n, (top, total, summed) in zip(both, results):
                tops[n] = top
                totals[n] = total
                acc[n] = summed
            return carry

        first = jnp.where(phase == 0, 1, 0)
        end = jnp.where(phase == 0, jnp.where(helper, 3, jnp.where(inner, 2, 1)), 1)
        lax.fori_loop(first, end, one_pair, 0)

    def own_sends(phase, direction):
        for part in (2 * phase, 2 * phase + 1):
            if direction == "left":
                start_all(to_left, part)
            else:
                start_all(to_right, part)

    for part in range(4):
        for load in loads[part]:
            load.wait()
        phase = part // 2
        if phase == 0:
            @pl.when(chip > low)
            def _():
                start_all(to_left, part)

            @pl.when(chip < high)
            def _():
                start_all(to_right, part)

            @pl.when(inner)
            def _():
                start_all(to_mate, part)
        else:
            @pl.when(((chip <= low) & (chip > 0)) | (chip == last))
            def _():
                start_all(to_left, part)

            @pl.when(((chip >= high) & (chip < last)) | (chip == 0))
            def _():
                start_all(to_right, part)

            start_all(to_mate, part)

    for head in range(heads):
        tile, at = divmod(head, heads_per_tile)
        qs[tile, at * new_rows:(at + 1) * new_rows, :] = q_ref[:, head * HEAD_DIM:(head + 1) * HEAD_DIM]
    tops[...] = jnp.full_like(tops, MASKED)
    totals[...] = jnp.zeros_like(totals)
    acc[...] = jnp.zeros_like(acc)

    @pl.when(helper)
    def _():
        q_copy.wait_recv()
        for head in range(heads // 2):
            tile, at = divmod(head, heads_per_tile)
            qs[4 + tile, at * new_rows:(at + 1) * new_rows, :] = q_in[:, head * HEAD_DIM:(head + 1) * HEAD_DIM]

    def take(at_chip, first_phase, phases):
        def one(n, carry):
            block = at_chip * 2 + jnp.where(n % 2 == 0, core, 1 - core)
            phase = first_phase + n // 2

            @pl.when(goes_mate(phase))
            def _():
                @pl.when(n % 2 == 1)
                def _():
                    for part in range(2):
                        for piece in range(PIECES):
                            to_mate(block, 2 * phase + part, piece).wait_recv()

                compute(block, phase)
            return carry
        lax.fori_loop(0, 2 * phases, one, 0)

    take(chip, 0, 1)

    def from_left(turn):
        late = turn - 2 * ahead
        phase = jnp.where(helped_right, 1, jnp.where(turn <= behind, 0, 1))
        step = jnp.where(helped_right, late, jnp.where(turn <= behind, turn, turn - behind))
        return (step >= 1) & (step <= behind), chip - step, phase

    def from_right(turn):
        late = turn - 2 * behind
        phase = jnp.where(helped_left, 1, jnp.where(turn <= ahead, 0, 1))
        step = jnp.where(helped_left, late, jnp.where(turn <= ahead, turn, turn - ahead))
        return (step >= 1) & (step <= ahead), chip + step, phase

    def pass_on(turn, half):
        for piece in range(PIECES):
            for coming, onward, goes in (
                (from_left, to_right, goes_right), (from_right, to_left, goes_left)):
                there, at_chip, phase = coming(turn)
                block, part = at_chip * 2 + core, 2 * phase + half

                @pl.when(there)
                def _():
                    to_mate(block, part, piece).wait_recv()

                    @pl.when(goes(phase))
                    def _():
                        onward(block, part, piece).start()

                    @pl.when(goes_mate(phase))
                    def _():
                        to_mate(block, part, piece).start()

    turns = max(2 * high, chips + HELPED)
    answered = chips - HELPED

    def one_turn(turn, carry):
        pass_on(turn, 0)

        @pl.when(helper & (turn == answered + 1))
        def _():
            o_copy.start()

        there, at_chip, phase = from_left(turn - 1)

        @pl.when(there | (turn == 1))
        def _():
            take(jnp.where(turn == 1, chip, at_chip), jnp.where(turn == 1, 1, phase), 1)

        pass_on(turn, 1)

        @pl.when((turn == behind) & (chip < high))
        def _():
            own_sends(1, "right")

        @pl.when((turn == ahead) & (chip > low))
        def _():
            own_sends(1, "left")

        there, at_chip, phase = from_right(turn - 1)

        @pl.when(there & (turn > 1))
        def _():
            take(at_chip, phase, 1)

        @pl.when(helper & (turn == answered))
        def _():
            for n in range(2):
                put(o_out, n, 4 + n)

        @pl.when(inner & (turn == answered + 1))
        def _():
            for n in range(2, 4):
                put(out_ref, n, n)
        return carry

    def put(target, place, tile):
        result = jnp.transpose(acc[tile] / totals[tile]).astype(jnp.bfloat16)
        for at in range(heads_per_tile):
            head = place * heads_per_tile + at
            target[:, head * HEAD_DIM:(head + 1) * HEAD_DIM] = result[at * new_rows:(at + 1) * new_rows]

    lax.fori_loop(1, turns + 2, one_turn, 0)

    for n in range(2):
        put(out_ref, n, n)

    @pl.when(helped)
    def _():
        o_copy.wait_recv()
        out_ref[:, half_width:] = o_in[...]
        q_copy.wait_send()

    @pl.when(helper)
    def _():
        o_copy.wait_send()

    def finish(n, carry):
        at_chip, part = n // 4, n % 4
        phase = part // 2
        block = at_chip * 2 + core

        @pl.when(goes_left(phase) & (at_chip >= chip))
        def _():
            to_left(block, part).wait_send()

        @pl.when(goes_right(phase) & (at_chip <= chip))
        def _():
            to_right(block, part).wait_send()

        @pl.when(goes_mate(phase))
        def _():
            to_mate(block, part).wait_send()
        return carry

    lax.fori_loop(0, 4 * chips, finish, 0)


def local(queries, cache_keys, cache_values, new_keys, new_values, prefix_len):
    count = lax.axis_size("ctx")
    chips = count // 2
    rows, width = queries.shape
    key_rows = cache_keys.shape[0] + new_keys.shape[0]
    tiles = 6
    dma = pltpu.SemaphoreType.DMA
    anywhere = pl.BlockSpec(memory_space=pl.ANY)
    return pl.pallas_call(
        functools.partial(kernel, chips),
        out_shape=jax.ShapeDtypeStruct((rows, width), jnp.bfloat16),
        in_specs=[pl.BlockSpec(memory_space=pltpu.SMEM), pl.BlockSpec(memory_space=pltpu.VMEM)] + [anywhere] * 4,
        out_specs=pl.BlockSpec(memory_space=pltpu.VMEM),
        scratch_shapes=[
            pltpu.VMEM((count, 4, key_rows, HEAD_DIM), jnp.bfloat16),
            pltpu.VMEM((tiles, TILE, HEAD_DIM), jnp.bfloat16),
            pltpu.VMEM((tiles, 1, TILE), jnp.float32),
            pltpu.VMEM((tiles, 1, TILE), jnp.float32),
            pltpu.VMEM((tiles, HEAD_DIM, TILE), jnp.float32),
            pltpu.VMEM((rows, width // 2), jnp.bfloat16),
            pltpu.VMEM((rows, width // 2), jnp.bfloat16),
            pltpu.VMEM((rows, width // 2), jnp.bfloat16),
            dma((8,)), dma((chips, 4)), dma((chips, 4)), dma((chips, 4)), dma((count, 4 * PIECES)),
            dma((2,)), dma((2,)),
        ],
        compiler_params=pltpu.CompilerParams(collective_id=0, has_side_effects=True),
    )(prefix_len, queries, cache_keys, cache_values, new_keys, new_values)


def solution(mesh):
    spec = P(("dp", "ctx"), "tp")
    return jax.shard_map(
        local, mesh=mesh, in_specs=(spec,) * 5 + (P("dp"),), out_specs=spec, check_vma=False)
```
